256 devices in a mesh: cls: 32 (over x, y, core), prt: 8 (over z).
Axes of the slice: x: 4, y: 4, z: 8, core: 2. Of those that a mesh axis runs over, the one named last changes fastest.
Arguments:
- particles: bfloat16 [4096, 128, 512], P(('cls', 'prt')), may hold values from -20100 to 20100
- references: bfloat16 [512, 128, 512], P('cls'), may hold values from -6 to 6
- owner_groups: int32 [4096, 4], P(('cls', 'prt')), may hold values from 0 to 31, all different within a row; in each aligned block of 16 rows (0 to 15, 16 to 31, ...) at most 4 rows name the same one
- class_order: int32 [4096, 4, 16], P(('cls', 'prt')), may hold values from 0 to 15, each once within a row
Outputs:
- class_sums: float32 [512, 128, 512], P('cls', 'prt')
- class_weights: float32 [512], P('cls')
- log_norm: float32 [4096], P(('cls', 'prt'))
The draws below stay inside these ranges and needn't reach their ends.
Inputs may be any that keep to these rules, and one draw needn't show every extreme that they name: `owner_groups`: each row names 4 different groups. Among the 16 particles of one device, no group is named by more than 4 rows, a bound that some block reaches. `class_order`: each row along the last dimension is a permutation.
All inputs are finite; a program needn't handle non-finite values.
Results may differ from the reference program's by a relative error of at most 0.0029.
Values may be sent and summed in bfloat16 or wider, within the bound.
A program may use at most 128 MiB of HBM per device.

```python
import math
import jax
import jax.numpy as jnp
import numpy as np
from jax import lax

CYCLES = 128
HARM = 256
CLASSES = 512
ROTS = 36
OWN_TOP = 4
CAND_OWN = 4
PART_DEV = 16
CLS_DEV = 16
CAP = 4
PARTICLES = 4096
N_CLS = 32


def draw_particles(key, part):
    base = jnp.clip(jax.random.normal(key, (PARTICLES, CYCLES, 2 * HARM), jnp.float32), -6.0, 6.0)
    return base.astype(jnp.bfloat16)


def draw_references(key, part):
    keys = jax.random.split(jax.random.fold_in(key, 31), 4)
    level = jnp.exp(jax.random.uniform(keys[0], (CYCLES,), jnp.float32, -0.3, 0.3))
    level = level / jnp.sqrt(jnp.mean(level * level))
    base = jnp.clip(jax.random.normal(keys[3], (CLASSES, CYCLES, 2 * HARM), jnp.float32), -4.0, 4.0)
    return (base * level[None, :, None]).astype(jnp.bfloat16)


def assign_block(key, own, number, rows, count, top, reach, slope):
    sequence = jax.random.permutation(key, count)
    packed, common = load_shares(count, rows * top, reach, slope, True), load_shares(count, rows * top, reach, slope, False)
    places = jnp.arange(count)

    def named(lengths, rotation):
        used = int((lengths > 0).sum())
        fixed = max(1, used // 4)
        moved = fixed + (places - fixed + rotation * (used - fixed)) % max(1, count - fixed)
        return jnp.zeros((count,), jnp.int32).at[sequence[jnp.where(places < fixed, places, moved)]].set(jnp.asarray(lengths, jnp.int32))

    lengths = jnp.where(number % 4 == 0, named(packed, number // 4), named(common, number - number // 4 - 1))
    mixed = jax.random.permutation(jax.random.fold_in(own, 3), count)
    source_of, taker = mixed[0:count // 2 * 2:2], mixed[1:count // 2 * 2:2]
    room = jnp.minimum(lengths[source_of] - 1, reach - lengths[taker]) // 2
    room = jnp.where((source_of == sequence[0]) | (taker == sequence[0]) | (lengths[taker] == 0), 0, jnp.maximum(room, 0))
    moved = jax.random.randint(jax.random.fold_in(own, 4), (count // 2,), 0, 1 << 20) % (room + 1)
    lengths = lengths.at[source_of].add(-moved).at[taker].add(moved)
    items = jnp.searchsorted(jnp.cumsum(lengths), jnp.arange(rows * top), side="right").astype(jnp.int32)
    table = items.reshape(top, rows).T
    table = table[jax.random.permutation(jax.random.fold_in(own, 1), rows)]
    rotation = jax.random.randint(jax.random.fold_in(own, 2), (rows, 1), 0, top)
    return jnp.take_along_axis(table, (jnp.arange(top)[None, :] + rotation) % top, axis=1)


def load_shares(count, total, limit, slope, full):
    weights = [(1 << 20) // math.isqrt(standing ** slope) + 1 for standing in range(1, count + 1)]
    largest = limit if full else min(limit, max(-(-total // count), total * weights[0] // sum(weights)))
    least = 1 if total - largest >= count - 1 else 0
    given, surplus = [largest] + [least] * (count - 1), total - largest - least * (count - 1)
    while surplus > 0:
        free = [i for i in range(1, count) if given[i] < largest] or [i for i in range(1, count) if given[i] < limit]
        mass, left = sum([weights[i] for i in free]), surplus
        for i in free:
            more = min(limit - given[i], max(1, left * weights[i] // mass), surplus)
            given[i] = given[i] + more
            surplus = surplus - more
    return np.array(given)


def setup_inputs(seed: int = 0) -> dict:
    streams_of = jax.random.split(jax.random.key(seed), 5)
    particles = draw_particles(jax.random.fold_in(streams_of[4], 71), 0)
    references = draw_references(jax.random.fold_in(streams_of[4], 71), 0)
    owner_groups_keys = jax.random.split(jax.random.fold_in(streams_of[2], 1), PARTICLES // PART_DEV)
    owner_groups_turns = jax.random.permutation(jax.random.fold_in(streams_of[2], 3), PARTICLES // PART_DEV)
    owner_groups = jax.vmap(lambda own, number: assign_block(jax.random.fold_in(streams_of[2], 2), own, number, PART_DEV, N_CLS, OWN_TOP, CAP, 2))(owner_groups_keys, owner_groups_turns).reshape((PARTICLES, OWN_TOP))
    class_order = jax.vmap(lambda own: jax.random.permutation(own, CLS_DEV))(jax.random.split(streams_of[3], PARTICLES * OWN_TOP)).reshape((PARTICLES, OWN_TOP, CLS_DEV)).astype(jnp.int32)
    return {"particles": particles, "references": references, "owner_groups": owner_groups, "class_order": class_order}


def reference(particles, references, owner_groups, class_order):
    groups = CLASSES // N_CLS
    total_cand = OWN_TOP * CAND_OWN
    candidates = (owner_groups[:, :, None] * groups + class_order[:, :, :CAND_OWN]).reshape(PARTICLES, total_cand).astype(jnp.int32)
    harmonic = jnp.arange(HARM, dtype=jnp.float32)
    angles = 2.0 * math.pi * jnp.arange(ROTS, dtype=jnp.float32) / ROTS
    phase = harmonic[:, None] * angles[None, :]
    forward = jnp.concatenate([jnp.cos(phase), jnp.sin(phase)], 0)
    backward = jnp.concatenate([jnp.cos(phase), -jnp.sin(phase)], 0).T
    scale = 2.0 / math.sqrt(CYCLES * 2 * HARM)
    norms = lax.optimization_barrier(jnp.sum(jnp.square(references.astype(jnp.float32)), axis=(1, 2)))
    block = 16
    steps = PARTICLES // block
    part_blocks = particles.reshape(steps, block, CYCLES, 2 * HARM)
    cand_blocks = candidates.reshape(steps, block, total_cand)

    def one_block(carry, inputs):
        sums, weights = carry
        span_part, span_cls = inputs
        chosen = references[span_cls].astype(jnp.float32)
        lanes = span_part.astype(jnp.float32)
        p_re = lanes[..., :HARM]
        p_im = lanes[..., HARM:]
        r_re = chosen[..., :HARM]
        r_im = chosen[..., HARM:]
        x_re = jnp.einsum('brm,bjrm->bjm', p_re, r_re) + jnp.einsum('brm,bjrm->bjm', p_im, r_im)
        x_im = jnp.einsum('brm,bjrm->bjm', p_im, r_re) - jnp.einsum('brm,bjrm->bjm', p_re, r_im)
        cross = jnp.concatenate([x_re, x_im], -1)
        corr = jnp.dot(cross.reshape(-1, 2 * HARM), forward, precision=lax.Precision.HIGHEST).reshape(block, total_cand, ROTS)
        score = (corr - 0.5 * norms[span_cls][:, :, None]) * scale
        top = lax.optimization_barrier(jnp.max(score, axis=(1, 2)))
        lse = top + jnp.log(lax.optimization_barrier(jnp.sum(jnp.exp(score - top[:, None, None]), axis=(1, 2))))
        weight = jnp.exp(score - lse[:, None, None])
        mixed = jnp.dot(weight.reshape(-1, ROTS), backward, precision=lax.Precision.HIGHEST).astype(jnp.bfloat16)
        mixed = lax.optimization_barrier(mixed).astype(jnp.float32).reshape(block, total_cand, 2 * HARM)
        y_re = mixed[:, :, None, :HARM]
        y_im = mixed[:, :, None, HARM:]
        s_re = p_re[:, None] * y_re - p_im[:, None] * y_im
        s_im = p_re[:, None] * y_im + p_im[:, None] * y_re
        added = jnp.concatenate([s_re, s_im], -1).reshape(block * total_cand, CYCLES, 2 * HARM)
        flat_cls = span_cls.reshape(-1)
        sums = sums.at[flat_cls].add(added)
        weights = weights.at[flat_cls].add(lax.optimization_barrier(jnp.sum(weight, axis=2)).reshape(-1))
        return ((sums, weights), lse)
    start = (jnp.zeros((CLASSES, CYCLES, 2 * HARM), jnp.float32), jnp.zeros((CLASSES,), jnp.float32))
    (sums, weights), norm_blocks = lax.scan(one_block, start, (part_blocks, cand_blocks))
    return (sums, weights, norm_blocks.reshape(PARTICLES))
```

```python
import functools
import math

import jax
import jax.numpy as jnp
from jax import lax
from jax.experimental import pallas as pl
from jax.experimental.pallas import tpu as pltpu
from jax.sharding import PartitionSpec as P

CYCLES = 128
HARM = 256
ROTS = 36
OWN_TOP = 4
CAND_OWN = 4
VMEM = pltpu.VMEM


def spectral_tables():
    harmonic = jnp.arange(HARM, dtype=jnp.float32)
    angles = 2.0 * math.pi * jnp.arange(ROTS, dtype=jnp.float32) / ROTS
    phase = harmonic[:, None] * angles[None, :]
    forward = jnp.concatenate([jnp.cos(phase), jnp.sin(phase)], 0)
    backward = jnp.concatenate([jnp.cos(phase), -jnp.sin(phase)], 0).T
    return (forward, backward)


def cross_kernel(cands, cand_ref, p_ref, r_ref, fwd_ref, corr_ref, cross, normrow, norms):
    n_part = p_ref.shape[0]

    @pl.loop(0, r_ref.shape[0] // 8)
    def _(b):
        rows = []
        for i in range(8):
            r = r_ref[b * 8 + i].astype(jnp.float32)
            s = jnp.sum(r * r, axis=0, keepdims=True)
            s = s[:, :HARM] + s[:, HARM:]
            rows.append(s[:, :128] + s[:, 128:])
        norms[pl.ds(b * 8, 8), :] = jnp.broadcast_to(
            0.5 * jnp.sum(jnp.concatenate(rows, 0), axis=1, keepdims=True), (8, 128)
        )

    @pl.loop(0, n_part)
    def _(n):
        p = p_ref[n].astype(jnp.float32)
        p_re, p_im = p[:, :HARM], p[:, HARM:]
        for j in range(cands):
            c = cand_ref[n * cands + j]
            r = r_ref[c].astype(jnp.float32)
            r_re, r_im = r[:, :HARM], r[:, HARM:]
            a = p_re * r_re + p_im * r_im
            b = p_im * r_re - p_re * r_im
            cross[pl.ds(n * cands + j, 1), :HARM] = jnp.sum(a, axis=0, keepdims=True)
            cross[pl.ds(n * cands + j, 1), HARM:] = jnp.sum(b, axis=0, keepdims=True)
            normrow[pl.ds(n * cands + j, 1), :] = norms[pl.ds(c, 1), :]

    @pl.loop(0, cross.shape[0] // 256)
    def _(b):
        rows = pl.ds(pl.multiple_of(b * 256, 256), 256)
        corr_ref[rows, :] = (
            jnp.dot(cross[rows, :], fwd_ref[...], precision=lax.Precision.HIGHEST)
            - normrow[rows, :]
        )


def sums_kernel(cands, cand_ref, p_ref, w_ref, bwd_ref, acc_ref, accw_ref, mixed):
    n_part = p_ref.shape[0]

    @pl.loop(0, mixed.shape[0] // 256)
    def _(b):
        rows = pl.ds(pl.multiple_of(b * 256, 256), 256)
        mixed[rows, :] = (
            jnp.dot(w_ref[rows, :], bwd_ref[...], precision=lax.Precision.HIGHEST)
            .astype(jnp.bfloat16)
            .astype(jnp.float32)
        )

    @pl.loop(0, acc_ref.shape[0])
    def _(c):
        acc_ref[c] = jnp.zeros(acc_ref.shape[1:], jnp.float32)

    accw_ref[...] = jnp.zeros_like(accw_ref)

    @pl.loop(0, n_part)
    def _(n):
        p = p_ref[n].astype(jnp.float32)
        p_re, p_im = p[:, :HARM], p[:, HARM:]
        for j in range(cands):
            c = cand_ref[n * cands + j]
            y = mixed[pl.ds(n * cands + j, 1), :]
            y_re, y_im = y[:, :HARM], y[:, HARM:]
            acc_ref[c, :, :HARM] += p_re * y_re - p_im * y_im
            acc_ref[c, :, HARM:] += p_re * y_im + p_im * y_re
            accw_ref[pl.ds(c, 1), :] += w_ref[pl.ds(n * cands + j, 1), :]


def per_device(particles, references, owner_groups, class_order):
    n_prt = lax.axis_size("prt")
    z = lax.axis_index("prt")
    count = particles.shape[0]
    groups = references.shape[0]
    width = 2 * HARM
    depth = CYCLES // n_prt
    cands = OWN_TOP * CAND_OWN
    total = count * n_prt
    classes = groups * lax.axis_size("cls")
    scale = 2.0 / math.sqrt(CYCLES * width)
    forward, backward = spectral_tables()
    fwd = jnp.pad(forward, ((0, 0), (0, 128 - ROTS)))
    bwd = jnp.pad(backward, ((0, 128 - ROTS), (0, 0)))

    own_cand = (owner_groups[:, :, None] * groups + class_order[:, :, :CAND_OWN]).reshape(-1)
    cand = lax.all_gather(own_cand, "prt", axis=0, tiled=True)
    column = lax.all_to_all(
        particles.reshape(count, n_prt, depth, width), "prt", split_axis=1, concat_axis=0, tiled=True
    ).reshape(total, depth, width)
    slab = lax.dynamic_slice_in_dim(references, z * depth, depth, axis=1)
    refs = lax.all_gather(slab, "cls", axis=0, tiled=True)

    corr = pl.pallas_call(
        functools.partial(cross_kernel, cands),
        out_shape=jax.ShapeDtypeStruct((total * cands, 128), jnp.float32),
        in_specs=[pl.BlockSpec(memory_space=pltpu.SMEM)] + [pl.BlockSpec(memory_space=VMEM)] * 3,
        out_specs=pl.BlockSpec(memory_space=VMEM),
        scratch_shapes=[
            VMEM((total * cands, width), jnp.float32),
            VMEM((total * cands, 128), jnp.float32),
            VMEM((classes, 128), jnp.float32),
        ],
        compiler_params=pltpu.CompilerParams(vmem_limit_bytes=60 * 2**20),
    )(cand, column, refs, fwd)
    mine = lax.psum_scatter(corr[:, :ROTS], "prt", scatter_dimension=0, tiled=True)
    score = mine.reshape(count, cands * ROTS) * scale
    top = jnp.max(score, axis=1, keepdims=True)
    log_norm = top + jnp.log(jnp.sum(jnp.exp(score - top), axis=1, keepdims=True))
    weight = jnp.exp(score - log_norm).reshape(count * cands, ROTS)
    weights = lax.all_gather(weight, "prt", axis=0, tiled=True)
    sums, sums_w = pl.pallas_call(
        functools.partial(sums_kernel, cands),
        out_shape=(
            jax.ShapeDtypeStruct((classes, depth, width), jnp.float32),
            jax.ShapeDtypeStruct((classes, 128), jnp.float32),
        ),
        in_specs=[pl.BlockSpec(memory_space=pltpu.SMEM)] + [pl.BlockSpec(memory_space=VMEM)] * 3,
        out_specs=[pl.BlockSpec(memory_space=VMEM)] * 2,
        scratch_shapes=[VMEM((total * cands, width), jnp.float32)],
        compiler_params=pltpu.CompilerParams(vmem_limit_bytes=60 * 2**20),
    )(cand, column, jnp.pad(weights, ((0, 0), (0, 128 - ROTS))), bwd)
    class_sums = lax.psum_scatter(sums, "cls", scatter_dimension=0, tiled=True)
    class_weights = lax.psum_scatter(
        jnp.sum(sums_w, axis=1), "cls", scatter_dimension=0, tiled=True
    )
    return (class_sums, class_weights, log_norm.reshape(count))


def solution(mesh):
    in_specs = (
        P(("cls", "prt"), None, None),
        P("cls", None, None),
        P(("cls", "prt"), None),
        P(("cls", "prt"), None, None),
    )
    out_specs = (P("cls", "prt", None), P("cls"), P(("cls", "prt")))
    return jax.shard_map(
        per_device, mesh=mesh, in_specs=in_specs, out_specs=out_specs, check_vma=False
    )
```

```python
import functools
import math

import jax
import jax.numpy as jnp
import numpy as np
from jax import lax
from jax.experimental import pallas as pl
from jax.experimental.pallas import tpu as pltpu
from jax.sharding import PartitionSpec as P

CYCLES = 128
HARM = 256
WIDTH = 2 * HARM
ROTS = 36
OWN_TOP = 4
CAND_OWN = 4
CANDS = OWN_TOP * CAND_OWN
ANG = 40
EXT = WIDTH + 128
VMEM, SMEM, ANY = pltpu.VMEM, pltpu.SMEM, pl.ANY
F32, BF16 = jnp.float32, jnp.bfloat16
DMA = pltpu.SemaphoreType.DMA
SCALE = 2.0 / math.sqrt(CYCLES * WIDTH)


def split3(x):
    high = x.astype(jnp.bfloat16).astype(np.float32)
    mid = (x - high).astype(jnp.bfloat16).astype(np.float32)
    low = (x - high - mid).astype(jnp.bfloat16).astype(np.float32)
    return high, mid, low


def spectral_tables():
    harmonic = np.arange(HARM, dtype=np.float32)
    angles = np.float32(2.0 * math.pi) * np.arange(ROTS, dtype=np.float32) / np.float32(ROTS)
    phase = (harmonic[:, None] * angles[None, :]).astype(np.float64)
    cos, sin = np.cos(phase).astype(np.float32).T, np.sin(phase).astype(np.float32).T
    forward = np.zeros((ANG, EXT), np.float32)
    forward[:ROTS, :HARM], forward[:ROTS, HARM:WIDTH] = cos, sin
    forward[:ROTS, WIDTH:] = -0.5
    backward = np.zeros((ANG, EXT), np.float32)
    backward[:ROTS, :HARM], backward[:ROTS, HARM:WIDTH] = cos, -sin
    backward[:ROTS, WIDTH:] = 1.0
    f_high, f_mid, f_low = split3(forward)
    b_high, b_mid, b_low = split3(backward)
    fwd = np.concatenate([f_high, f_mid, f_low, np.zeros((8, EXT), np.float32)], 0)
    bwd = np.concatenate([b_high, b_high, b_high, b_mid, b_mid, b_low], 0)
    return jnp.asarray(fwd, BF16), jnp.asarray(bwd, BF16)


def parts3(x):
    high = x.astype(BF16)
    rest = x - high.astype(F32)
    mid = rest.astype(BF16)
    low = (rest - mid.astype(F32)).astype(BF16)
    return high, mid, low


def row_sums(vs):
    row = lax.broadcasted_iota(jnp.int32, vs[0].shape, 0)
    for step in (1, 2, 4):
        keep = (row % (2 * step)) < step
        vs = [
            jnp.where(keep, a, b) + pltpu.roll(jnp.where(keep, b, a), 8 - step, 0)
            for a, b in zip(vs[0::2], vs[1::2])
        ]
    return vs[0]


def group_all(x, op):
    lane = lax.broadcasted_iota(jnp.int32, x.shape, 1)
    n = x.shape[1]
    for step in (1, 2, 4, 8):
        other = jnp.where(
            (lane // step) % 2 == 0, pltpu.roll(x, n - step, 1), pltpu.roll(x, step, 1)
        )
        x = op(x, other)
    return x


def where_am_i():
    cls = lax.axis_index("cls")
    return cls // 8, (cls // 2) % 4, cls % 2, lax.axis_index("prt")


def cls_of(x, y, core):
    return (x % 4) * 8 + (y % 4) * 2 + core


def remote(src, dst, send, recv, cls, prt):
    return pltpu.make_async_remote_copy(
        src, dst, send, recv, device_id=(cls, prt), device_id_type=pl.DeviceIdType.MESH
    )


def greet(peers):
    barrier = pltpu.get_barrier_semaphore()
    for cls, prt in peers:
        pl.semaphore_signal(
            barrier, inc=1, device_id=(cls, prt), device_id_type=pl.DeviceIdType.MESH
        )
    pl.semaphore_wait(barrier, len(peers))


def assign_kernel(
    part, refs, cand, fwd,
    halves, weights, cand_out, lse_out,
    pbuf, rbuf, cbuf, csm, cross, normrow, norms, cout, cin, wown,
    lsem, psend, precv, csend, crecv, r1send, r1recv, r2send, r2recv, rsend, rrecv,
    csem_s, csem_r, wsend, wrecv, xsend, xrecv,
):
    x, y, core, z = where_am_i()
    me = cls_of(x, y, core)
    mate = cls_of(x, y, 1 - core)
    greet(
        [(me, (z + d) % 8) for d in range(1, 8)]
        + [(cls_of(x + d, y, core), z) for d in range(1, 4)]
        + [(cls_of(x, y + d, core), z) for d in range(1, 4)]
        + [(mate, z)]
    )
    order = (1, 7, 2, 6, 3, 5, 4)

    c_cp = [remote(cand, cbuf.at[z], csend.at[d], crecv.at[d], me, (z + d) % 8) for d in order]
    for cp in c_cp:
        cp.start()

    def slab(g):
        return rbuf.at[pl.ds(g * 16, 16)]

    def half(g, k):
        return rbuf.at[pl.ds(g * 16 + 8 * k, 8)]

    r_cp = []
    for d in (1, 3, 2):
        r_cp.append(remote(refs.at[:, z], slab(me), r1send.at[d - 1], r1recv.at[d - 1], cls_of(x + d, y, core), z))
        r_cp.append(remote(refs.at[:, z], slab(me), r1send.at[d + 2], r1recv.at[d + 2], cls_of(x, y + d, core), z))
    r_cp.append(remote(refs.at[:, z], slab(me), rsend.at[0], rrecv.at[0], mate, z))
    p_cp = [remote(part.at[:, (z + d) % 8], pbuf.at[z], psend.at[d], precv.at[d], me, (z + d) % 8) for d in order]
    for cp in r_cp + p_cp:
        cp.start()
    own = [
        pltpu.make_async_copy(cand, cbuf.at[z], lsem.at[0]),
        pltpu.make_async_copy(refs.at[:, z], slab(me), lsem.at[1]),
        pltpu.make_async_copy(part.at[:, z], pbuf.at[z], lsem.at[2]),
    ]
    for cp in own:
        cp.start()

    sent = []

    def pass_on(ref, send, recv, cls):
        cp = remote(ref, ref, send, recv, cls, z)
        cp.start()
        sent.append(cp)

    for d in (1, 3, 2):
        g = cls_of(x - d + 4, y, core)
        remote(slab(g), slab(g), r1send.at[d - 1], r1recv.at[d - 1], me, z).wait_recv()
        for e in (1, 3, 2):
            k = (d - 1) * 3 + e - 1
            pass_on(half(g, 0), r2send.at[0, k], r2recv.at[0, k], cls_of(x, y + e, core))
        pass_on(slab(g), rsend.at[4 * d], rrecv.at[4 * d], mate)
        g = cls_of(x, y - d + 4, core)
        remote(slab(g), slab(g), r1send.at[d + 2], r1recv.at[d + 2], me, z).wait_recv()
        for e in (1, 3, 2):
            k = (e - 1) * 3 + d - 1
            pass_on(half(g, 1), r2send.at[1, k], r2recv.at[1, k], cls_of(x + e, y, core))
        pass_on(slab(g), rsend.at[d], rrecv.at[d], mate)
    for dx in (1, 3, 2):
        for dy in (1, 3, 2):
            k = (dx - 1) * 3 + dy - 1
            g = cls_of(x - dx + 4, y - dy + 4, core)
            for h in range(2):
                remote(half(g, h), half(g, h), r2send.at[h, k], r2recv.at[h, k], me, z).wait_recv()
            pass_on(slab(g), rsend.at[4 * dx + dy], rrecv.at[4 * dx + dy], mate)
    for cp in own:
        cp.wait()
    for d in order:
        remote(cbuf.at[(z - d + 8) % 8], cbuf.at[(z - d + 8) % 8], csend.at[d], crecv.at[d], me, z).wait_recv()
    scp = pltpu.make_async_copy(cbuf, csm, lsem.at[3])
    scp.start()
    for dx in range(4):
        for dy in range(4):
            g = cls_of(x - dx + 4, y - dy + 4, 1 - core)
            k = 4 * dx + dy
            remote(slab(g), slab(g), rsend.at[k], rrecv.at[k], me, z).wait_recv()
    scp.wait()
    c_back = pltpu.make_async_copy(cbuf, cand_out.at[core], lsem.at[0])
    c_back.start()
    c_mate = remote(cbuf, cand_out.at[core], xsend.at[8], xrecv.at[8], mate, z)
    c_mate.start()

    @pl.loop(0, 64)
    def _(b):
        vs = []
        for i in range(8):
            r = rbuf[b * 8 + i].astype(F32)
            s = jnp.sum(r * r, axis=0)
            s = s[:, :HARM] + s[:, HARM:]
            vs.append(s[:, :128] + s[:, 128:])
        norms[pl.ds(pl.multiple_of(b * 8, 8), 8), :] = row_sums(vs)

    @pl.loop(0, 8)
    def _(t):
        d = (t % 2) * ((t + 1) // 2) + (1 - t % 2) * ((8 - t // 2) % 8)
        src = (z - d + 8) % 8

        @pl.when(t > 0)
        def _():
            remote(pbuf.at[src], pbuf.at[src], psend.at[d], precv.at[d], me, z).wait_recv()

        @pl.loop(0, 16)
        def _(i):
            p = pbuf[src, i].astype(F32)
            p_re, p_im = p[:, :, :HARM], p[:, :, HARM:]
            for j0 in (0, 8):
                re, im = [], []
                row = pl.multiple_of(i * CANDS + j0, 8)
                for j in range(8):
                    c = csm[src, (i * CANDS + j0 + j) // 128, (i * CANDS + j0 + j) % 128]
                    r = rbuf[c].astype(F32)
                    r_re, r_im = r[:, :, :HARM], r[:, :, HARM:]
                    re.append(jnp.sum(p_re * r_re + p_im * r_im, axis=0))
                    im.append(jnp.sum(p_im * r_re - p_re * r_im, axis=0))
                    normrow[pl.ds(i * CANDS + j0 + j, 1), :] = norms[pl.ds(c, 1), :]
                cross[pl.ds(row, 8), :HARM] = row_sums(re)
                cross[pl.ds(row, 8), HARM:WIDTH] = row_sums(im)

        cross[:, WIDTH:] = normrow[...]
        total = jnp.zeros((ANG, 256), F32)
        for part3 in parts3(cross[...]):
            out = lax.dot_general(
                fwd[...], part3, (((1,), (1,)), ((), ())), preferred_element_type=F32
            )
            total = total + (out[:ANG] + (out[ANG : 2 * ANG] + out[2 * ANG : 3 * ANG]))
        cout[d] = total

        @pl.when(t > 0)
        def _():
            remote(cout.at[d], cin.at[d], csem_s.at[d], csem_r.at[d], me, src).start()

    halves_cp = pltpu.make_async_copy(pbuf.at[:, :, core], halves.at[core], lsem.at[2])
    halves_cp.start()
    halves_mate = remote(pbuf.at[:, :, 1 - core], halves.at[core], xsend.at[9], xrecv.at[9], mate, z)
    halves_mate.start()
    corr = cout[0]
    for d in range(1, 8):
        remote(cin.at[d], cin.at[d], csem_s.at[d], csem_r.at[d], me, z).wait_recv()
        corr = corr + cin[d]
    angle = lax.broadcasted_iota(jnp.int32, (ANG, 128), 0)
    for lanes in (slice(0, 128), slice(128, 256)):
        score = jnp.where(angle < ROTS, corr[:, lanes] * SCALE, -1e30)
        top = group_all(jnp.broadcast_to(jnp.max(score, axis=0, keepdims=True), (8, 128)), jnp.maximum)
        expo = jnp.where(angle < ROTS, jnp.exp(score - top[:1]), 0.0)
        den = group_all(jnp.broadcast_to(jnp.sum(expo, axis=0, keepdims=True), (8, 128)), jnp.add)
        lse = top + jnp.log(den)
        lse_out[:, lanes] = lse
        wown[:, lanes] = jnp.where(angle < ROTS, jnp.exp(score - lse[:1]), 0.0)
    w_cp = [
        remote(wown, weights.at[core, z], wsend.at[d], wrecv.at[d], me, (z + d) % 8) for d in order
    ]
    w_cp.append(remote(wown, weights.at[core, z], xsend.at[0], xrecv.at[0], mate, z))
    for cp in w_cp:
        cp.start()
    w_own = pltpu.make_async_copy(wown, weights.at[core, z], lsem.at[1])
    w_own.start()
    for d in order:
        land = weights.at[core, (z - d + 8) % 8]
        remote(land, land, wsend.at[d], wrecv.at[d], me, z).wait_recv()
        pass_on(land, xsend.at[d], xrecv.at[d], mate)

    for d in range(8):
        land = weights.at[1 - core, (z - d + 8) % 8]
        remote(land, land, xsend.at[d], xrecv.at[d], me, z).wait_recv()
    remote(cbuf, cand_out.at[1 - core], xsend.at[8], xrecv.at[8], me, z).wait_recv()
    remote(pbuf.at[:, :, core], halves.at[1 - core], xsend.at[9], xrecv.at[9], me, z).wait_recv()
    for cp in (w_own, c_back, halves_cp):
        cp.wait()
    for cp in c_cp + r_cp + p_cp + sent + [c_mate, halves_mate] + w_cp:
        cp.wait_send()
    for d in range(1, 8):
        remote(cout.at[d], cin.at[d], csem_s.at[d], csem_r.at[d], me, z).wait_send()


def sums_kernel(cand, halves, w_ref, bwd, out_ref, tot_ref, mixed, acc, accw):
    @pl.loop(0, 16)
    def _(b):
        w = w_ref[b // 8, b % 8]
        high, mid, low = [v.astype(F32) for v in parts3(w)]
        lhs = jnp.concatenate([high, mid, low, high, mid, high], 0).astype(BF16)
        y = lax.dot_general(
            lhs, bwd[...], (((0,), (0,)), ((), ())), preferred_element_type=F32
        )
        rows = pl.ds(pl.multiple_of(b * 256, 256), 256)
        mixed[rows, :WIDTH] = y[:, :WIDTH].astype(BF16).astype(F32)
        mixed[rows, WIDTH:] = y[:, WIDTH:]

    @pl.loop(0, acc.shape[0] // 8)
    def _(c):
        acc[pl.ds(c * 8, 8)] = jnp.zeros((8, 8, WIDTH), F32)

    accw[...] = jnp.zeros_like(accw)

    @pl.loop(0, 256)
    def _(n):
        p = halves[n // 128, (n // 16) % 8, n % 16].astype(F32)
        p_re, p_im = p[:, :HARM], p[:, HARM:]
        for j0 in range(0, CANDS, 4):
            cs, new, neww = [], [], []
            for j in range(4):
                pair = n * CANDS + j0 + j
                c = cand[n // 128, (n // 16) % 8, (pair // 128) % 2, pair % 128]
                row = mixed[pl.ds(pair, 1), :]
                y_re, y_im = row[:, :HARM], row[:, HARM:WIDTH]
                cs.append(c)
                new.append(
                    (
                        acc[c, :, :HARM] + (p_re * y_re - p_im * y_im),
                        acc[c, :, HARM:] + (p_re * y_im + p_im * y_re),
                    )
                )
                neww.append(accw[pl.ds(c, 1), :] + row[:, WIDTH:])
            for c, (re, im), tot in zip(cs, new, neww):
                acc[c, :, :HARM] = re
                acc[c, :, HARM:] = im
                accw[pl.ds(c, 1), :] = tot

    @pl.loop(0, acc.shape[0] // 8)
    def _(c):
        out_ref[pl.ds(c * 8, 8)] = acc[pl.ds(c * 8, 8)].astype(BF16)

    diag = lax.broadcasted_iota(jnp.int32, (128, 128), 0) == lax.broadcasted_iota(
        jnp.int32, (128, 128), 1
    )
    rows = [
        jnp.sum(jnp.where(diag, accw[128 * b : 128 * b + 128, :], 0.0), axis=0, keepdims=True)
        for b in range(4)
    ]
    tot_ref[...] = jnp.concatenate(rows + [jnp.zeros((4, 128), F32)], 0)


def scatter_kernel(
    part, tot,
    out_ref, tot_out,
    a1, b1, s2, r2, fin, totin,
    lsem, s1send, s1recv, s2send, s2recv, tsend, trecv, xsend, xrecv,
):
    x, y, core, z = where_am_i()
    me = cls_of(x, y, core)
    mate = cls_of(x, y, 1 - core)
    offsets = [(dx, dy) for dx in range(4) for dy in range(4) if dx or dy]
    greet([(cls_of(x + dx, y + dy, core), z) for dx, dy in offsets] + [(mate, z)])
    t_cp = [
        remote(tot, totin.at[4 * dx + dy], tsend.at[4 * dx + dy], trecv.at[4 * dx + dy], cls_of(x + dx, y + dy, core), z)
        for dx, dy in offsets
    ]
    cps = []
    for d in (2, 1, 3):
        cps.append(remote(part.at[(x + d) % 4, :, 0], a1.at[d], s1send.at[0, d], s1recv.at[0, d], cls_of(x + d, y, core), z))
        cps.append(remote(part.at[:, (y + d) % 4, 1], b1.at[d], s1send.at[1, d], s1recv.at[1, d], cls_of(x, y + d, core), z))
    for cp in t_cp + cps:
        cp.start()
    own = [
        pltpu.make_async_copy(part.at[x, :, 0], a1.at[0], lsem.at[0]),
        pltpu.make_async_copy(part.at[:, y, 1], b1.at[0], lsem.at[1]),
    ]
    for cp in own:
        cp.start()
    for cp in own:
        cp.wait()
    for k, land in enumerate((a1, b1)):
        for d in range(1, 4):
            remote(land.at[d], land.at[d], s1send.at[k, d], s1recv.at[k, d], me, z).wait_recv()
        mine = (y, x)[k]
        for d in (2, 1, 3, 0):
            to = (mine + d) % 4

            @pl.loop(0, 16)
            def _(q, d=d, to=to, land=land, k=k):
                total = (land[0, to, q].astype(F32) + land[1, to, q].astype(F32)) + (
                    land[2, to, q].astype(F32) + land[3, to, q].astype(F32)
                )
                if d:
                    s2[k, d, q] = total.astype(BF16)
                else:
                    fin[k, q] = total

            if d:
                dest = (cls_of(x, y + d, core), cls_of(x + d, y, core))[k]
                cp = remote(s2.at[k, d], r2.at[k, d], s2send.at[k, d], s2recv.at[k, d], dest, z)
                cp.start()
                cps.append(cp)
    for k in range(2):
        for d in range(1, 4):
            remote(r2.at[k, d], r2.at[k, d], s2send.at[k, d], s2recv.at[k, d], me, z).wait_recv()

        @pl.loop(0, 16)
        def _(q, k=k):
            fin[k, q] = fin[k, q] + (
                (r2[k, 1, q].astype(F32) + r2[k, 2, q].astype(F32)) + r2[k, 3, q].astype(F32)
            )

    cross_cp = remote(fin.at[1 - core], out_ref.at[:, core], xsend.at[0], xrecv.at[0], mate, z)
    cross_cp.start()
    keep = pltpu.make_async_copy(fin.at[core], out_ref.at[:, core], lsem.at[0])
    keep.start()
    total = tot[...]
    for dx, dy in offsets:
        k = 4 * dx + dy
        remote(totin.at[k], totin.at[k], tsend.at[k], trecv.at[k], me, z).wait_recv()
        total = total + totin[k]
    tot_out[...] = total
    remote(fin.at[core], out_ref.at[:, 1 - core], xsend.at[0], xrecv.at[0], me, z).wait_recv()
    keep.wait()
    for cp in t_cp + cps + [cross_cp]:
        cp.wait_send()


def spec(space):
    return pl.BlockSpec(memory_space=space)


def sds(shape, dtype):
    return jax.ShapeDtypeStruct(shape, dtype)


def per_device(particles, references, owner_groups, class_order):
    count = particles.shape[0]
    groups = references.shape[0]
    core = lax.axis_index("cls") % 2
    place = lax.axis_index("cls") % 8 // 2 * 32 + core * 16
    fwd, bwd = spectral_tables()
    own_cand = (owner_groups[:, :, None] * groups + class_order[:, :, :CAND_OWN]).reshape(2, 128)

    halves, weights, cand, lse = pl.pallas_call(
        assign_kernel,
        out_shape=(
            sds((2, 8, 16, 8, WIDTH), BF16),
            sds((2, 8, ANG, 256), F32),
            sds((2, 8, 2, 128), jnp.int32),
            sds((8, 256), F32),
        ),
        in_specs=[spec(ANY), spec(ANY), spec(VMEM), spec(VMEM)],
        out_specs=[spec(ANY), spec(ANY), spec(ANY), spec(VMEM)],
        scratch_shapes=[
            VMEM((8, 16, 2, 8, WIDTH), BF16),
            VMEM((512, 2, 8, WIDTH), BF16),
            VMEM((8, 2, 128), jnp.int32),
            SMEM((8, 2, 128), jnp.int32),
            VMEM((256, EXT), F32),
            VMEM((256, 128), F32),
            VMEM((512, 128), F32),
            VMEM((8, ANG, 256), F32),
            VMEM((8, ANG, 256), F32),
            VMEM((ANG, 256), F32),
            DMA((4,)), DMA((8,)), DMA((8,)), DMA((8,)), DMA((8,)), DMA((6,)), DMA((6,)),
            DMA((2, 9)), DMA((2, 9)), DMA((16,)), DMA((16,)), DMA((8,)), DMA((8,)),
            DMA((8,)), DMA((8,)), DMA((10,)), DMA((10,)),
        ],
        compiler_params=pltpu.CompilerParams(
            collective_id=0, has_side_effects=True, vmem_limit_bytes=48 * 2**20
        ),
    )(
        particles.reshape(count, 8, 2, 8, WIDTH),
        references.reshape(groups, 8, 2, 8, WIDTH),
        own_cand,
        fwd,
    )
    sums, totals = pl.pallas_call(
        sums_kernel,
        out_shape=(sds((512, 8, WIDTH), BF16), sds((8, 128), F32)),
        in_specs=[spec(SMEM), spec(VMEM), spec(VMEM), spec(VMEM)],
        out_specs=[spec(VMEM), spec(VMEM)],
        scratch_shapes=[
            VMEM((4096, EXT), F32),
            VMEM((512, 8, WIDTH), F32),
            VMEM((512, 128), F32),
        ],
        compiler_params=pltpu.CompilerParams(vmem_limit_bytes=56 * 2**20),
    )(cand, halves, weights, bwd)
    class_sums, class_tot = pl.pallas_call(
        scatter_kernel,
        out_shape=(sds((16, 2, 8, WIDTH), F32), sds((8, 128), F32)),
        in_specs=[spec(ANY), spec(VMEM)],
        out_specs=[spec(VMEM), spec(VMEM)],
        scratch_shapes=[
            VMEM((4, 4, 16, 8, WIDTH), BF16),
            VMEM((4, 4, 16, 8, WIDTH), BF16),
            VMEM((2, 4, 16, 8, WIDTH), BF16),
            VMEM((2, 4, 16, 8, WIDTH), BF16),
            VMEM((2, 16, 8, WIDTH), F32),
            VMEM((16, 8, 128), F32),
            DMA((2,)), DMA((2, 4)), DMA((2, 4)), DMA((2, 4)), DMA((2, 4)),
            DMA((16,)), DMA((16,)), DMA((1,)), DMA((1,)),
        ],
        compiler_params=pltpu.CompilerParams(
            collective_id=1, has_side_effects=True, vmem_limit_bytes=48 * 2**20
        ),
    )(sums.reshape(4, 4, 2, 16, 8, WIDTH), totals)
    row = lax.dynamic_index_in_dim(class_tot, lax.axis_index("cls") // 8, 0, keepdims=False)
    class_weights = lax.dynamic_slice_in_dim(row, place, 16)
    log_norm = lse[0].reshape(count, CANDS)[:, 0]
    return (class_sums.reshape(groups, 16, WIDTH), class_weights, log_norm)


def solution(mesh):
    in_specs = (
        P(("cls", "prt"), None, None),
        P("cls", None, None),
        P(("cls", "prt"), None),
        P(("cls", "prt"), None, None),
    )
    out_specs = (P("cls", "prt", None), P("cls"), P(("cls", "prt")))
    return jax.shard_map(
        per_device, mesh=mesh, in_specs=in_specs, out_specs=out_specs, check_vma=False
    )
```

```python
import functools
import math

import jax
import jax.numpy as jnp
import numpy as np
from jax import lax
from jax.experimental import pallas as pl
from jax.experimental.pallas import tpu as pltpu
from jax.sharding import PartitionSpec as P

CYCLES = 128
HARM = 256
WIDTH = 2 * HARM
ROTS = 36
OWN_TOP = 4
CAND_OWN = 4
CANDS = OWN_TOP * CAND_OWN
ANG = 40
EXT = WIDTH + 128
VMEM, SMEM, ANY = pltpu.VMEM, pltpu.SMEM, pl.ANY
F32, BF16 = jnp.float32, jnp.bfloat16
DMA = pltpu.SemaphoreType.DMA
SCALE = 2.0 / math.sqrt(CYCLES * WIDTH)


def split3(x):
    high = x.astype(jnp.bfloat16).astype(np.float32)
    mid = (x - high).astype(jnp.bfloat16).astype(np.float32)
    low = (x - high - mid).astype(jnp.bfloat16).astype(np.float32)
    return high, mid, low


def spectral_tables():
    harmonic = np.arange(HARM, dtype=np.float32)
    angles = np.float32(2.0 * math.pi) * np.arange(ROTS, dtype=np.float32) / np.float32(ROTS)
    phase = (harmonic[:, None] * angles[None, :]).astype(np.float64)
    cos, sin = np.cos(phase).astype(np.float32).T, np.sin(phase).astype(np.float32).T
    forward = np.zeros((ANG, EXT), np.float32)
    forward[:ROTS, :HARM], forward[:ROTS, HARM:WIDTH] = cos, sin
    forward[:ROTS, WIDTH:] = -0.5
    backward = np.zeros((ANG, EXT), np.float32)
    backward[:ROTS, :HARM], backward[:ROTS, HARM:WIDTH] = cos, -sin
    backward[:ROTS, WIDTH:] = 1.0
    f_high, f_mid, f_low = split3(forward)
    b_high, b_mid, b_low = split3(backward)
    fwd = np.concatenate([f_high, f_mid, f_low, np.zeros((8, EXT), np.float32)], 0)
    bwd = np.concatenate([b_high, b_high, b_high, b_mid, b_mid, b_low], 0)
    return jnp.asarray(fwd, BF16), jnp.asarray(bwd, BF16)


def parts3(x):
    high = x.astype(BF16)
    rest = x - high.astype(F32)
    mid = rest.astype(BF16)
    low = (rest - mid.astype(F32)).astype(BF16)
    return high, mid, low


def row_sums(vs):
    row = lax.broadcasted_iota(jnp.int32, vs[0].shape, 0)
    for step in (1, 2, 4):
        keep = (row % (2 * step)) < step
        vs = [
            jnp.where(keep, a, b) + pltpu.roll(jnp.where(keep, b, a), 8 - step, 0)
            for a, b in zip(vs[0::2], vs[1::2])
        ]
    return vs[0]


def group_all(x, op):
    lane = lax.broadcasted_iota(jnp.int32, x.shape, 1)
    n = x.shape[1]
    for step in (1, 2, 4, 8):
        other = jnp.where(
            (lane // step) % 2 == 0, pltpu.roll(x, n - step, 1), pltpu.roll(x, step, 1)
        )
        x = op(x, other)
    return x


def where_am_i():
    cls = lax.axis_index("cls")
    return cls // 8, (cls // 2) % 4, cls % 2, lax.axis_index("prt")


def cls_of(x, y, core):
    return (x % 4) * 8 + (y % 4) * 2 + core


def remote(src, dst, send, recv, cls, prt):
    return pltpu.make_async_remote_copy(
        src, dst, send, recv, device_id=(cls, prt), device_id_type=pl.DeviceIdType.MESH
    )


def greet(peers):
    barrier = pltpu.get_barrier_semaphore()
    for cls, prt in peers:
        pl.semaphore_signal(
            barrier, inc=1, device_id=(cls, prt), device_id_type=pl.DeviceIdType.MESH
        )
    pl.semaphore_wait(barrier, len(peers))


def assign_kernel(
    part, refs, cand, fwd_hbm,
    halves, weights, cand_out, lse_out,
    pbuf, rbuf, rcomb, cbuf, csm, cross, normrow, norms, cout, cin, wown, fwd, lsem, ssem, rsem,
):
    x, y, core, z = where_am_i()
    me = cls_of(x, y, core)
    mate = cls_of(x, y, 1 - core)
    greet(
        [(me, (z + d) % 8) for d in range(1, 8)]
        + [(cls_of(x + d, y, core), z) for d in (1, 3)]
        + [(cls_of(x, y + d, core), z) for d in (1, 3)]
        + [(mate, z)]
    )
    around = (1, 7, 2, 6, 3, 5, 4)

    def at(dx, dy, col=None):
        return cls_of(x - dx + 4, y - dy + 4, core if col is None else col)

    def go(dx, dy):
        return cls_of(x + dx + 4, y + dy + 4, core)

    def piece(g, start=0, size=16):
        return rbuf.at[pl.ds(g * 16 + start, size)]

    sent = []

    def send(src, dst, k, cls, prt):
        cp = remote(src, dst, ssem.at[k], rsem.at[k], cls, prt)
        cp.start()
        sent.append(cp)

    def pass_on(ref, k, cls):
        send(ref, ref, k, cls, z)

    def arrive(ref, k):
        remote(ref, ref, ssem.at[k], rsem.at[k], me, z).wait_recv()

    for d in around:
        send(cand, cbuf.at[z], d, me, (z + d) % 8)
    own_refs = refs.at[:, z]
    for k, dx, dy in ((16, 1, 0), (17, -1, 0), (18, 0, 1), (19, 0, -1)):
        send(own_refs, piece(me), k, go(dx, dy), z)
    send(own_refs, piece(me), 64, mate, z)
    for d in around:
        send(part.at[:, (z + d) % 8], pbuf.at[z], 80 + d, me, (z + d) % 8)
    own = [
        pltpu.make_async_copy(cand, cbuf.at[z], lsem.at[0]),
        pltpu.make_async_copy(own_refs, piece(me), lsem.at[1]),
        pltpu.make_async_copy(part.at[:, z], pbuf.at[z], lsem.at[2]),
    ]
    fwd_cp = pltpu.make_async_copy(fwd_hbm, fwd, lsem.at[4])
    for cp in own + [fwd_cp]:
        cp.start()

    def to_mate(dx, dy):
        pass_on(piece(at(dx, dy)), 64 + 4 * dx + dy, mate)

    for k, (dx, dy) in ((16, (1, 0)), (18, (0, 1)), (17, (3, 0)), (19, (0, 3))):
        g = at(dx, dy)
        arrive(piece(g), k)
        if dy == 0:
            pass_on(piece(g, 0 if dx == 1 else 8, 8), 20 + (dx == 3), go(2 - dx, 0))
            pass_on(piece(g, 0, 8), 24 + 2 * (dx - 1), go(0, 1))
            pass_on(piece(g, 0, 8), 25 + 2 * (dx - 1), go(0, -1))
        else:
            pass_on(piece(g, 0 if dy == 1 else 8, 8), 22 + (dy == 3), go(0, 2 - dy))
            pass_on(piece(g, 8, 8), 30 + 2 * (dy - 1), go(1, 0))
            pass_on(piece(g, 8, 8), 31 + 2 * (dy - 1), go(-1, 0))
        to_mate(dx, dy)
    g = at(2, 0)
    arrive(piece(g, 0, 8), 20)
    pass_on(piece(g, 0, 8), 26, go(0, 1))
    pass_on(piece(g, 0, 8), 27, go(0, -1))
    g = at(0, 2)
    arrive(piece(g, 8, 8), 23)
    pass_on(piece(g, 8, 8), 32, go(1, 0))
    pass_on(piece(g, 8, 8), 33, go(-1, 0))
    for m in (1, 3, 2):
        for side in range(2):
            dy = 1 + 2 * side
            g = at(m, dy)
            arrive(piece(g, 0, 8), 24 + 2 * (m - 1) + side)
            pass_on(piece(g, 4 * side, 4), 36 + 2 * (m - 1) + side, go(0, 1 - 2 * side))
            g = at(dy, m)
            arrive(piece(g, 8, 8), 30 + 2 * (m - 1) + side)
            pass_on(piece(g, 8 + 4 * side, 4), 42 + 2 * (m - 1) + side, go(1 - 2 * side, 0))
    arrive(piece(at(2, 0), 8, 8), 21)
    to_mate(2, 0)
    arrive(piece(at(0, 2), 0, 8), 22)
    to_mate(0, 2)
    for dx in (1, 3):
        for dy in (1, 3):
            to_mate(dx, dy)
    for m in (1, 3, 2):
        for side in range(2):
            arrive(piece(at(m, 2), 4 * side, 4), 36 + 2 * (m - 1) + side)
            arrive(piece(at(2, m), 8 + 4 * side, 4), 42 + 2 * (m - 1) + side)
        to_mate(m, 2)
        if m != 2:
            to_mate(2, m)
    for cp in own:
        cp.wait()
    for d in around:
        arrive(cbuf.at[(z - d + 8) % 8], d)
    scp = pltpu.make_async_copy(cbuf, csm, lsem.at[3])
    scp.start()
    c_back = pltpu.make_async_copy(cbuf, cand_out.at[core], lsem.at[0])
    c_back.start()
    send(cbuf, cand_out.at[core], 12, mate, z)

    def norms_of(g):
        @pl.loop(0, 2)
        def _(b):
            vs = []
            for i in range(8):
                k = g * 16 + b * 8 + i
                r = rbuf[k].astype(F32)
                re, im = r[:, :, :HARM], r[:, :, HARM:]
                rcomb[k, 0] = re
                rcomb[k, 1] = re + im
                rcomb[k, 2] = im - re
                s = jnp.sum(re * re + im * im, axis=0)
                vs.append(s[:, :128] + s[:, 128:])
            norms[pl.ds(pl.multiple_of(g * 16 + b * 8, 8), 8), :] = row_sums(vs)

    slices = [(0, 0), (1, 0), (0, 1), (3, 0), (0, 3), (2, 0), (0, 2), (1, 1), (1, 3), (3, 1), (3, 3)]
    slices += [(1, 2), (2, 1), (3, 2), (2, 3), (2, 2)]

    @pl.loop(0, 16)
    def _(k):
        norms_of(2 * k + core)

    for dx, dy in slices:
        arrive(piece(at(dx, dy, 1 - core)), 64 + 4 * dx + dy)

    @pl.loop(0, 16)
    def _(k):
        norms_of(2 * k + 1 - core)

    scp.wait()
    fwd_cp.wait()

    @pl.loop(0, 8)
    def _(t):
        d = (t % 2) * ((t + 1) // 2) + (1 - t % 2) * ((8 - t // 2) % 8)
        src = (z - d + 8) % 8

        @pl.when(t > 0)
        def _():
            arrive(pbuf.at[src], 80 + d)

        @pl.loop(0, 2)
        def _(hi):
            @pl.loop(0, 8)
            def _(lo):
                i = hi * 8 + lo
                p = pbuf[src, i].astype(F32)
                p_re, p_im = p[:, :, :HARM], p[:, :, HARM:]
                p_sum = p_re + p_im
                for j0 in (0, 8):
                    re, im = [], []
                    row = pl.multiple_of(i * CANDS + j0, 8)
                    for j in range(8):
                        c = csm[src, hi, lo * CANDS + (j0 + j)]
                        k1 = jnp.sum(p_sum * rcomb[c, 0], axis=0)
                        k2 = jnp.sum(p_re * rcomb[c, 1], axis=0)
                        k3 = jnp.sum(p_im * rcomb[c, 2], axis=0)
                        re.append(k1 + k3)
                        im.append(k1 - k2)
                        normrow[pl.ds(i * CANDS + j0 + j, 1), :] = norms[pl.ds(c, 1), :]
                    cross[pl.ds(row, 8), :HARM] = row_sums(re)
                    cross[pl.ds(row, 8), HARM:WIDTH] = row_sums(im)

        cross[:, WIDTH:] = normrow[...]
        total = jnp.zeros((ANG, 256), F32)
        for part3 in parts3(cross[...]):
            out = lax.dot_general(
                fwd[...], part3, (((1,), (1,)), ((), ())), preferred_element_type=F32
            )
            total = total + (out[:ANG] + (out[ANG : 2 * ANG] + out[2 * ANG : 3 * ANG]))
        cout[d] = total

        @pl.when(t > 0)
        def _():
            remote(cout.at[d], cin.at[d], ssem.at[88 + d], rsem.at[88 + d], me, src).start()

    halves_cp = pltpu.make_async_copy(pbuf.at[:, :, core], halves.at[core], lsem.at[2])
    halves_cp.start()
    send(pbuf.at[:, :, 1 - core], halves.at[core], 13, mate, z)
    corr = cout[0]
    for d in range(1, 8):
        arrive(cin.at[d], 88 + d)
        corr = corr + cin[d]
    angle = lax.broadcasted_iota(jnp.int32, (ANG, 128), 0)
    for lanes in (slice(0, 128), slice(128, 256)):
        score = jnp.where(angle < ROTS, corr[:, lanes] * SCALE, -1e30)
        top = group_all(jnp.broadcast_to(jnp.max(score, axis=0, keepdims=True), (8, 128)), jnp.maximum)
        expo = jnp.where(angle < ROTS, jnp.exp(score - top[:1]), 0.0)
        den = group_all(jnp.broadcast_to(jnp.sum(expo, axis=0, keepdims=True), (8, 128)), jnp.add)
        lse = top + jnp.log(den)
        lse_out[:, lanes] = lse
        wown[:, lanes] = jnp.where(angle < ROTS, jnp.exp(score - lse[:1]), 0.0)
    for d in around:
        send(wown, weights.at[core, z], 96 + d, me, (z + d) % 8)
    send(wown, weights.at[core, z], 104, mate, z)
    w_own = pltpu.make_async_copy(wown, weights.at[core, z], lsem.at[1])
    w_own.start()
    for d in (1, 7, 2, 6, 3, 5, 4):
        land = weights.at[core, (z - d + 8) % 8]
        arrive(land, 96 + d)
        pass_on(land, 104 + d, mate)

    for d in range(8):
        arrive(weights.at[1 - core, (z - d + 8) % 8], 104 + d)
    arrive(cand_out.at[1 - core], 12)
    arrive(halves.at[1 - core], 13)
    for cp in (w_own, c_back, halves_cp):
        cp.wait()
    for cp in sent:
        cp.wait_send()
    for d in range(1, 8):
        remote(cout.at[d], cin.at[d], ssem.at[88 + d], rsem.at[88 + d], me, z).wait_send()


def sums_kernel(
    cand, halves_hbm, w_hbm, bwd_hbm,
    out_ref, own_ref, tot_ref,
    halves, w_ref, bwd, mixed, tots, acc, accw, obuf, lsem, osem,
):
    x, y, _, _ = where_am_i()
    loads = [
        pltpu.make_async_copy(w_hbm, w_ref, lsem.at[0]),
        pltpu.make_async_copy(bwd_hbm, bwd, lsem.at[1]),
        pltpu.make_async_copy(halves_hbm, halves, lsem.at[2]),
    ]
    for cp in loads:
        cp.start()

    @pl.loop(0, acc.shape[0] // 8)
    def _(c):
        acc[pl.ds(c * 8, 8)] = jnp.zeros((8, 8, WIDTH), F32)

    accw[...] = jnp.zeros_like(accw)
    loads[0].wait()
    loads[1].wait()

    @pl.loop(0, 16)
    def _(b):
        w = w_ref[b // 8, b % 8]
        high, mid, low = [v.astype(F32) for v in parts3(w)]
        lhs = jnp.concatenate([high, mid, low, high, mid, high], 0).astype(BF16)
        y = lax.dot_general(
            lhs, bwd[...], (((0,), (0,)), ((), ())), preferred_element_type=F32
        )
        block = pl.ds(b * 16, 16)
        mixed[block] = y[:, :WIDTH].astype(BF16).astype(F32).reshape(16, CANDS, WIDTH)
        tots[block] = y[:, WIDTH:].reshape(16, CANDS, 128)

    loads[2].wait()

    @pl.loop(0, 32)
    def _(b):
        @pl.loop(0, 8)
        def _(lo):
            p = halves[b * 8 + lo].astype(F32)
            p_re, p_im = p[:, :HARM], p[:, HARM:]
            for j0 in range(0, CANDS, 8):
                cs, new, neww = [], [], []
                for j in range(j0, j0 + 8):
                    c = cand[b, lo * CANDS + j]
                    row = mixed[b * 8 + lo, pl.ds(j, 1), :]
                    y_re, y_im = row[:, :HARM], row[:, HARM:]
                    cs.append(c)
                    new.append(
                        (
                            acc[c, :, :HARM] + (p_re * y_re - p_im * y_im),
                            acc[c, :, HARM:] + (p_re * y_im + p_im * y_re),
                        )
                    )
                    neww.append(accw[pl.ds(c, 1), :] + tots[b * 8 + lo, pl.ds(j, 1), :])
                for c, (re, im), tot in zip(cs, new, neww):
                    acc[c, :, :HARM] = re
                    acc[c, :, HARM:] = im
                    accw[pl.ds(c, 1), :] = tot

    out = []
    for k in range(4):
        out.append(pltpu.make_async_copy(acc.at[pl.ds((x * 8 + k * 2) * 16, 16)], own_ref.at[0, k], osem.at[k]))
        out.append(pltpu.make_async_copy(acc.at[pl.ds((k * 8 + y * 2 + 1) * 16, 16)], own_ref.at[1, k], osem.at[4 + k]))
    for cp in out:
        cp.start()
    for k in range(4):

        @pl.loop(0, 16)
        def _(c, k=k):
            at = pl.ds(k * 128 + c * 8, 8)
            obuf[at] = acc[at].astype(BF16)

        at = pl.ds(k * 128, 128)
        out.append(pltpu.make_async_copy(obuf.at[at], out_ref.at[at], osem.at[8 + k]))
        out[-1].start()
    diag = lax.broadcasted_iota(jnp.int32, (128, 128), 0) == lax.broadcasted_iota(
        jnp.int32, (128, 128), 1
    )
    rows = [
        jnp.sum(jnp.where(diag, accw[128 * b : 128 * b + 128, :], 0.0), axis=0, keepdims=True)
        for b in range(4)
    ]
    tot_ref[...] = jnp.concatenate(rows + [jnp.zeros((4, 128), F32)], 0)
    for cp in out:
        cp.wait()


def scatter_kernel(
    part, own_hbm, tot,
    out_ref, tot_out,
    relay, direct, joined, mine, send3, own32, s2, r2, fin, totin,
    lsem, ssem, rsem, tsend, trecv,
):
    x, y, core, z = where_am_i()
    me = cls_of(x, y, core)
    mate = cls_of(x, y, 1 - core)
    offsets = [(dx, dy) for dx in range(4) for dy in range(4) if dx or dy]
    greet([(cls_of(x + dx, y + dy, core), z) for dx, dy in offsets] + [(mate, z)])
    sent = []

    def send(src, dst, k, cls):
        cp = remote(src, dst, ssem.at[k], rsem.at[k], cls, z)
        cp.start()
        sent.append(cp)

    def arrive(ref, k):
        remote(ref, ref, ssem.at[k], rsem.at[k], me, z).wait_recv()

    def sel(k, to, h):
        to = (to + 8) % 4
        return part.at[to, :, 0, h] if k == 0 else part.at[:, to, 1, h]

    def step(k, d, first):
        along_x = (k == 0) == first
        return cls_of(x + d + 4, y, core) if along_x else cls_of(x, y + d + 4, core)

    for dx, dy in offsets:
        k = 4 * dx + dy
        cp = remote(tot, totin.at[k], tsend.at[k], trecv.at[k], cls_of(x + dx, y + dy, core), z)
        cp.start()
        sent.append(cp)
    for k in range(2):
        u = (x, y)[k]
        send(sel(k, u + 2, 0), relay.at[k, 0], 8 * k, step(k, 1, True))
        send(sel(k, u + 2, 1), relay.at[k, 1], 8 * k + 1, step(k, -1, True))
    for k in range(2):
        u = (x, y)[k]
        send(sel(k, u + 1, 1), direct.at[k, 0], 8 * k + 2, step(k, 1, True))
        send(sel(k, u - 1, 0), direct.at[k, 1], 8 * k + 3, step(k, -1, True))
    loads = []
    for k in range(2):
        u = (x, y)[k]
        loads.append(pltpu.make_async_copy(sel(k, u + 1, 0), mine.at[k, 0], lsem.at[3 * k]))
        loads.append(pltpu.make_async_copy(sel(k, u - 1, 1), mine.at[k, 1], lsem.at[3 * k + 1]))
        loads.append(pltpu.make_async_copy(own_hbm.at[k], own32.at[k], lsem.at[3 * k + 2]))
    for cp in loads:
        cp.start()
    for cp in loads:
        cp.wait()
    rounds = (2, 1, 3, 0)
    for k in range(2):
        v = (y, x)[k]
        for side in range(2):
            arrive(relay.at[k, side], 8 * k + side)
        for e in rounds:
            w = (v + e) % 4
            for side in range(2):

                @pl.loop(0, 8)
                def _(q, k=k, w=w, side=side):
                    send3[k, side, w, q] = (
                        relay[k, side, w, q].astype(F32) + mine[k, side, w, q].astype(F32)
                    ).astype(BF16)

                n = 16 + 8 * k + 2 * e + side
                send(send3.at[k, side, w], joined.at[k, side, w], n, step(k, 1 - 2 * side, True))
    for k in range(2):
        for side in range(2):
            arrive(direct.at[k, side], 8 * k + 2 + side)
    for e in rounds:
        for k in range(2):
            v = (y, x)[k]
            w = (v + e) % 4
            for side in range(2):
                arrive(joined.at[k, side, w], 16 + 8 * k + 2 * e + side)

            @pl.loop(0, 8)
            def _(q, k=k, w=w, e=e):
                for side in range(2):
                    total = own32[k, w, side * 8 + q] + (
                        joined[k, side, w, q].astype(F32) + direct[k, 1 - side, w, q].astype(F32)
                    )
                    if e:
                        s2[k, e, side * 8 + q] = total.astype(BF16)
                    else:
                        fin[k, side * 8 + q] = total

            if e:
                send(s2.at[k, e], r2.at[k, e], 32 + 4 * k + e, step(k, e, False))
    for k in range(2):
        for e in (1, 2, 3):
            arrive(r2.at[k, e], 32 + 4 * k + e)

        @pl.loop(0, 16)
        def _(q, k=k):
            fin[k, q] = fin[k, q] + (
                (r2[k, 1, q].astype(F32) + r2[k, 2, q].astype(F32)) + r2[k, 3, q].astype(F32)
            )

    send(fin.at[1 - core], out_ref.at[:, core], 40, mate)
    keep = pltpu.make_async_copy(fin.at[core], out_ref.at[:, core], lsem.at[0])
    keep.start()
    total = tot[...]
    for dx, dy in offsets:
        k = 4 * dx + dy
        remote(totin.at[k], totin.at[k], tsend.at[k], trecv.at[k], me, z).wait_recv()
        total = total + totin[k]
    tot_out[...] = total
    arrive(out_ref.at[:, 1 - core], 40)
    keep.wait()
    for cp in sent:
        cp.wait_send()


def spec(space):
    return pl.BlockSpec(memory_space=space)


def sds(shape, dtype):
    return jax.ShapeDtypeStruct(shape, dtype)


def per_device(particles, references, owner_groups, class_order):
    count = particles.shape[0]
    groups = references.shape[0]
    core = lax.axis_index("cls") % 2
    place = lax.axis_index("cls") % 8 // 2 * 32 + core * 16
    fwd, bwd = spectral_tables()
    own_cand = (owner_groups[:, :, None] * groups + class_order[:, :, :CAND_OWN]).reshape(2, 128)

    halves, weights, cand, lse = pl.pallas_call(
        assign_kernel,
        out_shape=(
            sds((2, 8, 16, 8, WIDTH), BF16),
            sds((2, 8, ANG, 256), F32),
            sds((2, 8, 2, 128), jnp.int32),
            sds((8, 256), F32),
        ),
        in_specs=[spec(ANY), spec(ANY), spec(VMEM), spec(ANY)],
        out_specs=[spec(ANY), spec(ANY), spec(ANY), spec(VMEM)],
        scratch_shapes=[
            VMEM((8, 16, 2, 8, WIDTH), BF16),
            VMEM((512, 2, 8, WIDTH), BF16),
            VMEM((512, 3, 2, 8, HARM), F32),
            VMEM((8, 2, 128), jnp.int32),
            SMEM((8, 2, 128), jnp.int32),
            VMEM((256, EXT), F32),
            VMEM((256, 128), F32),
            VMEM((512, 128), F32),
            VMEM((8, ANG, 256), F32),
            VMEM((8, ANG, 256), F32),
            VMEM((ANG, 256), F32),
            VMEM((128, EXT), BF16),
            DMA((5,)), DMA((112,)), DMA((112,)),
        ],
        compiler_params=pltpu.CompilerParams(
            collective_id=0, has_side_effects=True, vmem_limit_bytes=48 * 2**20
        ),
    )(
        particles.reshape(count, 8, 2, 8, WIDTH),
        references.reshape(groups, 8, 2, 8, WIDTH),
        own_cand,
        fwd,
    )
    sums, own, totals = pl.pallas_call(
        sums_kernel,
        out_shape=(
            sds((512, 8, WIDTH), BF16),
            sds((2, 4, 16, 8, WIDTH), F32),
            sds((8, 128), F32),
        ),
        in_specs=[spec(SMEM), spec(ANY), spec(ANY), spec(ANY)],
        out_specs=[spec(ANY), spec(ANY), spec(VMEM)],
        scratch_shapes=[
            VMEM((256, 8, WIDTH), BF16),
            VMEM((2, 8, ANG, 256), F32),
            VMEM((6 * ANG, EXT), BF16),
            VMEM((256, CANDS, WIDTH), F32),
            VMEM((256, CANDS, 128), F32),
            VMEM((512, 8, WIDTH), F32),
            VMEM((512, 128), F32),
            VMEM((512, 8, WIDTH), BF16),
            DMA((3,)), DMA((12,)),
        ],
        compiler_params=pltpu.CompilerParams(vmem_limit_bytes=56 * 2**20),
    )(cand.reshape(32, 128), halves.reshape(256, 8, WIDTH), weights, bwd)
    class_sums, class_tot = pl.pallas_call(
        scatter_kernel,
        out_shape=(sds((16, 2, 8, WIDTH), F32), sds((8, 128), F32)),
        in_specs=[spec(ANY), spec(ANY), spec(VMEM)],
        out_specs=[spec(VMEM), spec(VMEM)],
        scratch_shapes=[VMEM((2, 2, 4, 8, 8, WIDTH), BF16)] * 5
        + [
            VMEM((2, 4, 16, 8, WIDTH), F32),
            VMEM((2, 4, 16, 8, WIDTH), BF16),
            VMEM((2, 4, 16, 8, WIDTH), BF16),
            VMEM((2, 16, 8, WIDTH), F32),
            VMEM((16, 8, 128), F32),
            DMA((6,)), DMA((41,)), DMA((41,)), DMA((16,)), DMA((16,)),
        ],
        compiler_params=pltpu.CompilerParams(
            collective_id=1, has_side_effects=True, vmem_limit_bytes=48 * 2**20
        ),
    )(sums.reshape(4, 4, 2, 2, 8, 8, WIDTH), own, totals)
    row = lax.dynamic_index_in_dim(class_tot, lax.axis_index("cls") // 8, 0, keepdims=False)
    class_weights = lax.dynamic_slice_in_dim(row, place, 16)
    log_norm = lse[0].reshape(count, CANDS)[:, 0]
    return (class_sums.reshape(groups, 16, WIDTH), class_weights, log_norm)


def solution(mesh):
    in_specs = (
        P(("cls", "prt"), None, None),
        P("cls", None, None),
        P(("cls", "prt"), None),
        P(("cls", "prt"), None, None),
    )
    out_specs = (P("cls", "prt", None), P("cls"), P(("cls", "prt")))
    return jax.shard_map(
        per_device, mesh=mesh, in_specs=in_specs, out_specs=out_specs, check_vma=False
    )
```

```python
import functools
import math

import jax
import jax.numpy as jnp
import numpy as np
from jax import lax
from jax.experimental import pallas as pl
from jax.experimental.pallas import tpu as pltpu
from jax.sharding import PartitionSpec as P

CYCLES = 128
HARM = 256
WIDTH = 2 * HARM
ROTS = 36
OWN_TOP = 4
CAND_OWN = 4
CANDS = OWN_TOP * CAND_OWN
ANG = 40
EXT = WIDTH + 128
VMEM, SMEM, HBM = pltpu.VMEM, pltpu.SMEM, pltpu.HBM
F32, BF16 = jnp.float32, jnp.bfloat16
DMA = pltpu.SemaphoreType.DMA
SCALE = 2.0 / math.sqrt(CYCLES * WIDTH)


def split3(x):
    high = x.astype(jnp.bfloat16).astype(np.float32)
    mid = (x - high).astype(jnp.bfloat16).astype(np.float32)
    low = (x - high - mid).astype(jnp.bfloat16).astype(np.float32)
    return high, mid, low


def spectral_tables():
    harmonic = np.arange(HARM, dtype=np.float32)
    angles = np.float32(2.0 * math.pi) * np.arange(ROTS, dtype=np.float32) / np.float32(ROTS)
    phase = (harmonic[:, None] * angles[None, :]).astype(np.float64)
    cos, sin = np.cos(phase).astype(np.float32).T, np.sin(phase).astype(np.float32).T
    forward = np.zeros((ANG, EXT), np.float32)
    forward[:ROTS, :HARM], forward[:ROTS, HARM:WIDTH] = cos, sin
    forward[:ROTS, WIDTH:] = -0.5
    backward = np.zeros((ANG, EXT), np.float32)
    backward[:ROTS, :HARM], backward[:ROTS, HARM:WIDTH] = cos, -sin
    backward[:ROTS, WIDTH:] = 1.0
    f_high, f_mid, f_low = split3(forward)
    b_high, b_mid, b_low = split3(backward)
    fwd = np.concatenate([f_high, f_mid, f_low, np.zeros((8, EXT), np.float32)], 0)
    bwd = np.concatenate([b_high, b_high, b_high, b_mid, b_mid, b_low], 0)
    return jnp.asarray(fwd, BF16), jnp.asarray(bwd, BF16)


def parts3(x):
    high = x.astype(BF16)
    rest = x - high.astype(F32)
    mid = rest.astype(BF16)
    low = (rest - mid.astype(F32)).astype(BF16)
    return high, mid, low


def row_sums(vs):
    row = lax.broadcasted_iota(jnp.int32, vs[0].shape, 0)
    for step in (1, 2, 4):
        keep = (row % (2 * step)) < step
        vs = [
            jnp.where(keep, a, b) + pltpu.roll(jnp.where(keep, b, a), 8 - step, 0)
            for a, b in zip(vs[0::2], vs[1::2])
        ]
    return vs[0]


def group_all(x, op):
    lane = lax.broadcasted_iota(jnp.int32, x.shape, 1)
    n = x.shape[1]
    for step in (1, 2, 4, 8):
        other = jnp.where(
            (lane // step) % 2 == 0, pltpu.roll(x, n - step, 1), pltpu.roll(x, step, 1)
        )
        x = op(x, other)
    return x


def where_am_i():
    cls = lax.axis_index("cls")
    return cls // 8, (cls // 2) % 4, cls % 2, lax.axis_index("prt")


def cls_of(x, y, core):
    return (x % 4) * 8 + (y % 4) * 2 + core


def remote(src, dst, send, recv, cls, prt):
    return pltpu.make_async_remote_copy(
        src, dst, send, recv, device_id=(cls, prt), device_id_type=pl.DeviceIdType.MESH
    )


def greet(peers):
    barrier = pltpu.get_barrier_semaphore()
    for cls, prt in peers:
        pl.semaphore_signal(
            barrier, inc=1, device_id=(cls, prt), device_id_type=pl.DeviceIdType.MESH
        )
    pl.semaphore_wait(barrier, len(peers))


def assign_kernel(
    part, refs, cand, fwd_hbm,
    halves, weights, cand_out, lse_out,
    pbuf, rbuf, rcomb, cbuf, csm, cross, normrow, norms, cout, cin, wown, fwd, lsem, ssem, rsem,
):
    x, y, core, z = where_am_i()
    me = cls_of(x, y, core)
    mate = cls_of(x, y, 1 - core)
    greet(
        [(me, (z + d) % 8) for d in range(1, 8)]
        + [(cls_of(x + d, y, core), z) for d in (1, 3)]
        + [(cls_of(x, y + d, core), z) for d in (1, 3)]
        + [(mate, z)]
    )
    around = (1, 7, 2, 6, 3, 5, 4)

    def at(dx, dy, col=None):
        return cls_of(x - dx + 4, y - dy + 4, core if col is None else col)

    def go(dx, dy):
        return cls_of(x + dx + 4, y + dy + 4, core)

    def piece(g, start=0, size=16):
        return rbuf.at[pl.ds(g * 16 + start, size)]

    sent = []

    def send(src, dst, k, cls, prt):
        cp = remote(src, dst, ssem.at[k], rsem.at[k], cls, prt)
        cp.start()
        sent.append(cp)

    def pass_on(ref, k, cls):
        send(ref, ref, k, cls, z)

    def arrive(ref, k):
        remote(ref, ref, ssem.at[k], rsem.at[k], me, z).wait_recv()

    for d in around:
        send(cand, cbuf.at[z], d, me, (z + d) % 8)
    own_refs = refs.at[:, z]
    for k, dx, dy in ((16, 1, 0), (17, -1, 0), (18, 0, 1), (19, 0, -1)):
        send(own_refs, piece(me), k, go(dx, dy), z)
    send(own_refs, piece(me), 64, mate, z)
    for h in range(2):
        for d in around:
            rows = pl.ds(8 * h, 8)
            send(part.at[rows, (z + d) % 8], pbuf.at[z, rows], 80 + 32 * h + d, me, (z + d) % 8)
    own = [
        pltpu.make_async_copy(cand, cbuf.at[z], lsem.at[0]),
        pltpu.make_async_copy(own_refs, piece(me), lsem.at[1]),
        pltpu.make_async_copy(part.at[:, z], pbuf.at[z], lsem.at[2]),
    ]
    fwd_cp = pltpu.make_async_copy(fwd_hbm, fwd, lsem.at[4])
    for cp in own + [fwd_cp]:
        cp.start()

    def to_mate(dx, dy):
        pass_on(piece(at(dx, dy)), 64 + 4 * dx + dy, mate)

    for k, (dx, dy) in ((16, (1, 0)), (18, (0, 1)), (17, (3, 0)), (19, (0, 3))):
        g = at(dx, dy)
        arrive(piece(g), k)
        if dy == 0:
            pass_on(piece(g, 0 if dx == 1 else 8, 8), 20 + (dx == 3), go(2 - dx, 0))
            pass_on(piece(g, 0, 8), 24 + 2 * (dx - 1), go(0, 1))
            pass_on(piece(g, 0, 8), 25 + 2 * (dx - 1), go(0, -1))
        else:
            pass_on(piece(g, 0 if dy == 1 else 8, 8), 22 + (dy == 3), go(0, 2 - dy))
            pass_on(piece(g, 8, 8), 30 + 2 * (dy - 1), go(1, 0))
            pass_on(piece(g, 8, 8), 31 + 2 * (dy - 1), go(-1, 0))
        to_mate(dx, dy)
    g = at(2, 0)
    arrive(piece(g, 0, 8), 20)
    pass_on(piece(g, 0, 8), 26, go(0, 1))
    pass_on(piece(g, 0, 8), 27, go(0, -1))
    g = at(0, 2)
    arrive(piece(g, 8, 8), 23)
    pass_on(piece(g, 8, 8), 32, go(1, 0))
    pass_on(piece(g, 8, 8), 33, go(-1, 0))
    for m in (1, 3, 2):
        for side in range(2):
            dy = 1 + 2 * side
            g = at(m, dy)
            arrive(piece(g, 0, 8), 24 + 2 * (m - 1) + side)
            pass_on(piece(g, 4 * side, 4), 36 + 2 * (m - 1) + side, go(0, 1 - 2 * side))
            g = at(dy, m)
            arrive(piece(g, 8, 8), 30 + 2 * (m - 1) + side)
            pass_on(piece(g, 8 + 4 * side, 4), 42 + 2 * (m - 1) + side, go(1 - 2 * side, 0))
    arrive(piece(at(2, 0), 8, 8), 21)
    to_mate(2, 0)
    arrive(piece(at(0, 2), 0, 8), 22)
    to_mate(0, 2)
    for dx in (1, 3):
        for dy in (1, 3):
            to_mate(dx, dy)
    for m in (1, 3, 2):
        for side in range(2):
            arrive(piece(at(m, 2), 4 * side, 4), 36 + 2 * (m - 1) + side)
            arrive(piece(at(2, m), 8 + 4 * side, 4), 42 + 2 * (m - 1) + side)
        to_mate(m, 2)
        if m != 2:
            to_mate(2, m)
    for cp in own:
        cp.wait()
    for d in around:
        arrive(cbuf.at[(z - d + 8) % 8], d)
    scp = pltpu.make_async_copy(cbuf, csm, lsem.at[3])
    scp.start()
    c_back = pltpu.make_async_copy(cbuf, cand_out.at[core], lsem.at[0])
    c_back.start()
    send(cbuf, cand_out.at[core], 12, mate, z)

    def norms_of(g):
        @pl.loop(0, 2)
        def _(b):
            vs = []
            for i in range(8):
                k = g * 16 + b * 8 + i
                r = rbuf[k].astype(F32)
                re, im = r[:, :, :HARM], r[:, :, HARM:]
                rcomb[k, 0] = re
                rcomb[k, 1] = re + im
                rcomb[k, 2] = im - re
                s = jnp.sum(re * re + im * im, axis=0)
                vs.append(s[:, :128] + s[:, 128:])
            norms[pl.ds(pl.multiple_of(g * 16 + b * 8, 8), 8), :] = row_sums(vs)

    slices = [(0, 0), (1, 0), (0, 1), (3, 0), (0, 3), (2, 0), (0, 2), (1, 1), (1, 3), (3, 1), (3, 3)]
    slices += [(1, 2), (2, 1), (3, 2), (2, 3), (2, 2)]

    @pl.loop(0, 16)
    def _(k):
        norms_of(2 * k + core)

    for dx, dy in slices:
        arrive(piece(at(dx, dy, 1 - core)), 64 + 4 * dx + dy)

    @pl.loop(0, 16)
    def _(k):
        norms_of(2 * k + 1 - core)

    scp.wait()
    fwd_cp.wait()

    angle = lax.broadcasted_iota(jnp.int32, (ANG, 128), 0)

    def score(h, first, last):
        @pl.loop(first, last)
        def _(t):
            d = (t % 2) * ((t + 1) // 2) + (1 - t % 2) * ((8 - t // 2) % 8)
            src = (z - d + 8) % 8

            @pl.when(t > 0)
            def _():
                arrive(pbuf.at[src, pl.ds(8 * h, 8)], 80 + 32 * h + d)

            @pl.loop(0, 8)
            def _(lo):
                p = pbuf[src, h * 8 + lo].astype(F32)
                p_re, p_im = p[:, :, :HARM], p[:, :, HARM:]
                p_sum = p_re + p_im
                for j0 in (0, 8):
                    re, im = [], []
                    row = pl.multiple_of(lo * CANDS + j0, 8)
                    for j in range(8):
                        c = csm[src, h, lo * CANDS + (j0 + j)]
                        k1 = jnp.sum(p_sum * rcomb[c, 0], axis=0)
                        k2 = jnp.sum(p_re * rcomb[c, 1], axis=0)
                        k3 = jnp.sum(p_im * rcomb[c, 2], axis=0)
                        re.append(k1 + k3)
                        im.append(k1 - k2)
                        normrow[pl.ds(lo * CANDS + j0 + j, 1), :] = norms[pl.ds(c, 1), :]
                    cross[pl.ds(row, 8), :HARM] = row_sums(re)
                    cross[pl.ds(row, 8), HARM:WIDTH] = row_sums(im)

            cross[:, WIDTH:] = normrow[...]
            total = jnp.zeros((ANG, 128), F32)
            for part3 in parts3(cross[...]):
                out = lax.dot_general(
                    fwd[...], part3, (((1,), (1,)), ((), ())), preferred_element_type=F32
                )
                total = total + (out[:ANG] + (out[ANG : 2 * ANG] + out[2 * ANG : 3 * ANG]))
            cout[h, d] = total

            @pl.when(t > 0)
            def _():
                k = 88 + 32 * h + d
                remote(cout.at[h, d], cin.at[h, d], ssem.at[k], rsem.at[k], me, src).start()

    def weigh(h):
        corr = cout[h, 0]
        for d in range(1, 8):
            arrive(cin.at[h, d], 88 + 32 * h + d)
            corr = corr + cin[h, d]
        score_h = jnp.where(angle < ROTS, corr * SCALE, -1e30)
        top = group_all(jnp.broadcast_to(jnp.max(score_h, axis=0, keepdims=True), (8, 128)), jnp.maximum)
        expo = jnp.where(angle < ROTS, jnp.exp(score_h - top[:1]), 0.0)
        den = group_all(jnp.broadcast_to(jnp.sum(expo, axis=0, keepdims=True), (8, 128)), jnp.add)
        lse = top + jnp.log(den)
        lse_out[:, 128 * h : 128 * h + 128] = lse
        wown[h] = jnp.where(angle < ROTS, jnp.exp(score_h - lse[:1]), 0.0)
        for d in around:
            send(wown.at[h], weights.at[core, z, h], 96 + 32 * h + d, me, (z + d) % 8)
        send(wown.at[h], weights.at[core, z, h], 104 + 32 * h, mate, z)

    score(0, 0, 8)
    score(1, 0, 8)
    weigh(0)
    halves_cp = pltpu.make_async_copy(pbuf.at[:, :, core], halves.at[core], lsem.at[2])
    halves_cp.start()
    send(pbuf.at[:, :, 1 - core], halves.at[core], 13, mate, z)
    weigh(1)
    w_own = pltpu.make_async_copy(wown, weights.at[core, z], lsem.at[1])
    w_own.start()
    for h in range(2):
        for d in around:
            land = weights.at[core, (z - d + 8) % 8, h]
            arrive(land, 96 + 32 * h + d)
            pass_on(land, 104 + 32 * h + d, mate)

    for h in range(2):
        for d in range(8):
            arrive(weights.at[1 - core, (z - d + 8) % 8, h], 104 + 32 * h + d)
    arrive(cand_out.at[1 - core], 12)
    arrive(halves.at[1 - core], 13)
    for cp in (w_own, c_back, halves_cp):
        cp.wait()
    for cp in sent:
        cp.wait_send()
    for h in range(2):
        for d in range(1, 8):
            k = 88 + 32 * h + d
            remote(cout.at[h, d], cin.at[h, d], ssem.at[k], rsem.at[k], me, z).wait_send()


def sums_kernel(
    cand_in, halves, w_ref, bwd_hbm,
    out_ref, acc, tot_ref,
    cand, bwd, mixed, tots, accw, lsem,
):
    loads = [
        pltpu.make_async_copy(bwd_hbm, bwd, lsem.at[0]),
        pltpu.make_async_copy(cand_in, cand, lsem.at[1]),
    ]
    for cp in loads:
        cp.start()

    @pl.loop(0, acc.shape[0] // 8)
    def _(c):
        acc[pl.ds(c * 8, 8)] = jnp.zeros((8, 8, WIDTH), F32)

    accw[...] = jnp.zeros_like(accw)
    for cp in loads:
        cp.wait()

    @pl.loop(0, 16)
    def _(b):
        w = jnp.concatenate([w_ref[b // 8, b % 8, 0], w_ref[b // 8, b % 8, 1]], 1)
        high, mid, low = [v.astype(F32) for v in parts3(w)]
        lhs = jnp.concatenate([high, mid, low, high, mid, high], 0).astype(BF16)
        y = lax.dot_general(
            lhs, bwd[...], (((0,), (0,)), ((), ())), preferred_element_type=F32
        )
        block = pl.ds(b * 16, 16)
        mixed[block] = y[:, :WIDTH].astype(BF16).astype(F32).reshape(16, CANDS, WIDTH)
        tots[block] = y[:, WIDTH:].reshape(16, CANDS, 128)

    @pl.loop(0, 32)
    def _(b):
        @pl.loop(0, 8)
        def _(lo):
            p = halves[b * 8 + lo].astype(F32)
            p_re, p_im = p[:, :HARM], p[:, HARM:]
            for j0 in range(0, CANDS, 8):
                cs, new, neww = [], [], []
                for j in range(j0, j0 + 8):
                    c = cand[b, lo * CANDS + j]
                    row = mixed[b * 8 + lo, pl.ds(j, 1), :]
                    y_re, y_im = row[:, :HARM], row[:, HARM:]
                    cs.append(c)
                    new.append(
                        (
                            acc[c, :, :HARM] + (p_re * y_re - p_im * y_im),
                            acc[c, :, HARM:] + (p_re * y_im + p_im * y_re),
                        )
                    )
                    neww.append(accw[pl.ds(c, 1), :] + tots[b * 8 + lo, pl.ds(j, 1), :])
                for c, (re, im), tot in zip(cs, new, neww):
                    acc[c, :, :HARM] = re
                    acc[c, :, HARM:] = im
                    accw[pl.ds(c, 1), :] = tot

    @pl.loop(0, 64)
    def _(c):
        out_ref[pl.ds(c * 8, 8)] = acc[pl.ds(c * 8, 8)].astype(BF16)

    diag = lax.broadcasted_iota(jnp.int32, (128, 128), 0) == lax.broadcasted_iota(
        jnp.int32, (128, 128), 1
    )
    rows = [
        jnp.sum(jnp.where(diag, accw[128 * b : 128 * b + 128, :], 0.0), axis=0, keepdims=True)
        for b in range(4)
    ]
    tot_ref[...] = jnp.concatenate(rows + [jnp.zeros((4, 128), F32)], 0)


def scatter_kernel(
    part, own, tot,
    out_ref, tot_out,
    relay, direct, joined, send3, s2, r2, fin, totin,
    lsem, ssem, rsem, tsend, trecv,
):
    x, y, core, z = where_am_i()
    me = cls_of(x, y, core)
    mate = cls_of(x, y, 1 - core)
    offsets = [(dx, dy) for dx in range(4) for dy in range(4) if dx or dy]
    greet([(cls_of(x + dx, y + dy, core), z) for dx, dy in offsets] + [(mate, z)])
    sent = []

    def send(src, dst, k, cls):
        cp = remote(src, dst, ssem.at[k], rsem.at[k], cls, z)
        cp.start()
        sent.append(cp)

    def arrive(ref, k):
        remote(ref, ref, ssem.at[k], rsem.at[k], me, z).wait_recv()

    def sel(k, to, h):
        to = (to + 8) % 4
        return part.at[to, :, 0, h] if k == 0 else part.at[:, to, 1, h]

    def step(k, d, first):
        along_x = (k == 0) == first
        return cls_of(x + d + 4, y, core) if along_x else cls_of(x, y + d + 4, core)

    for dx, dy in offsets:
        k = 4 * dx + dy
        cp = remote(tot, totin.at[k], tsend.at[k], trecv.at[k], cls_of(x + dx, y + dy, core), z)
        cp.start()
        sent.append(cp)
    for k in range(2):
        u = (x, y)[k]
        send(sel(k, u + 2, 0), relay.at[k, 0], 8 * k, step(k, 1, True))
        send(sel(k, u + 2, 1), relay.at[k, 1], 8 * k + 1, step(k, -1, True))
    for k in range(2):
        u = (x, y)[k]
        send(sel(k, u + 1, 1), direct.at[k, 0], 8 * k + 2, step(k, 1, True))
        send(sel(k, u - 1, 0), direct.at[k, 1], 8 * k + 3, step(k, -1, True))
    def partial(k, to, w, q):
        g = (to % 4) * 8 + w * 2 if k == 0 else w * 8 + (to % 4) * 2 + 1
        return own[g * 16 + q]

    rounds = (2, 1, 3, 0)
    for k in range(2):
        u, v = (x, y)[k], (y, x)[k]
        for side in range(2):
            arrive(relay.at[k, side], 8 * k + side)
        for e in rounds:
            w = (v + e) % 4
            for side in range(2):
                to = u + 1 + 2 * side

                @pl.loop(0, 8)
                def _(q, k=k, w=w, side=side, to=to):
                    send3[k, side, w, q] = (
                        relay[k, side, w, q].astype(F32) + partial(k, to, w, side * 8 + q)
                    ).astype(BF16)

                n = 16 + 8 * k + 2 * e + side
                send(send3.at[k, side, w], joined.at[k, side, w], n, step(k, 1 - 2 * side, True))
    for k in range(2):
        for side in range(2):
            arrive(direct.at[k, side], 8 * k + 2 + side)
    for e in rounds:
        for k in range(2):
            u, v = (x, y)[k], (y, x)[k]
            w = (v + e) % 4
            for side in range(2):
                arrive(joined.at[k, side, w], 16 + 8 * k + 2 * e + side)

            @pl.loop(0, 8)
            def _(q, k=k, u=u, w=w, e=e):
                for side in range(2):
                    total = partial(k, u, w, side * 8 + q) + (
                        joined[k, side, w, q].astype(F32) + direct[k, 1 - side, w, q].astype(F32)
                    )
                    if e:
                        s2[k, e, side * 8 + q] = total.astype(BF16)
                    else:
                        fin[k, side * 8 + q] = total

            if e:
                send(s2.at[k, e], r2.at[k, e], 32 + 4 * k + e, step(k, e, False))
    for k in range(2):
        for e in (1, 2, 3):
            arrive(r2.at[k, e], 32 + 4 * k + e)

        @pl.loop(0, 16)
        def _(q, k=k):
            fin[k, q] = fin[k, q] + (
                (r2[k, 1, q].astype(F32) + r2[k, 2, q].astype(F32)) + r2[k, 3, q].astype(F32)
            )

    send(fin.at[1 - core], out_ref.at[:, core], 40, mate)
    keep = pltpu.make_async_copy(fin.at[core], out_ref.at[:, core], lsem.at[0])
    keep.start()
    total = tot[...]
    for dx, dy in offsets:
        k = 4 * dx + dy
        remote(totin.at[k], totin.at[k], tsend.at[k], trecv.at[k], me, z).wait_recv()
        total = total + totin[k]
    tot_out[...] = total
    arrive(out_ref.at[:, 1 - core], 40)
    keep.wait()
    for cp in sent:
        cp.wait_send()


def spec(space):
    return pl.BlockSpec(memory_space=space)


def sds(shape, dtype):
    return jax.ShapeDtypeStruct(shape, dtype)


def per_device(particles, references, owner_groups, class_order):
    count = particles.shape[0]
    groups = references.shape[0]
    core = lax.axis_index("cls") % 2
    place = lax.axis_index("cls") % 8 // 2 * 32 + core * 16
    fwd, bwd = spectral_tables()
    own_cand = (owner_groups[:, :, None] * groups + class_order[:, :, :CAND_OWN]).reshape(2, 128)

    halves, weights, cand, lse = pl.pallas_call(
        assign_kernel,
        out_shape=(
            sds((2, 8, 16, 8, WIDTH), BF16),
            sds((2, 8, 2, ANG, 128), F32),
            sds((2, 8, 2, 128), jnp.int32),
            sds((8, 256), F32),
        ),
        in_specs=[spec(HBM), spec(HBM), spec(VMEM), spec(HBM)],
        out_specs=[spec(VMEM)] * 4,
        scratch_shapes=[
            VMEM((8, 16, 2, 8, WIDTH), BF16),
            VMEM((512, 2, 8, WIDTH), BF16),
            VMEM((512, 3, 2, 8, HARM), F32),
            VMEM((8, 2, 128), jnp.int32),
            SMEM((8, 2, 128), jnp.int32),
            VMEM((128, EXT), F32),
            VMEM((128, 128), F32),
            VMEM((512, 128), F32),
            VMEM((2, 8, ANG, 128), F32),
            VMEM((2, 8, ANG, 128), F32),
            VMEM((2, ANG, 128), F32),
            VMEM((128, EXT), BF16),
            DMA((5,)), DMA((144,)), DMA((144,)),
        ],
        compiler_params=pltpu.CompilerParams(
            collective_id=0, has_side_effects=True, vmem_limit_bytes=50 * 2**20
        ),
    )(
        particles.reshape(count, 8, 2, 8, WIDTH),
        references.reshape(groups, 8, 2, 8, WIDTH),
        own_cand,
        fwd,
    )
    sums, own, totals = pl.pallas_call(
        sums_kernel,
        out_shape=(
            sds((512, 8, WIDTH), BF16),
            sds((512, 8, WIDTH), F32),
            sds((8, 128), F32),
        ),
        in_specs=[spec(VMEM), spec(VMEM), spec(VMEM), spec(HBM)],
        out_specs=[spec(VMEM)] * 3,
        scratch_shapes=[
            SMEM((32, 128), jnp.int32),
            VMEM((6 * ANG, EXT), BF16),
            VMEM((256, CANDS, WIDTH), F32),
            VMEM((256, CANDS, 128), F32),
            VMEM((512, 128), F32),
            DMA((2,)),
        ],
        compiler_params=pltpu.CompilerParams(vmem_limit_bytes=20 * 2**20),
    )(cand.reshape(32, 128), halves.reshape(256, 8, WIDTH), weights, bwd)
    class_sums, class_tot = pl.pallas_call(
        scatter_kernel,
        out_shape=(sds((16, 2, 8, WIDTH), F32), sds((8, 128), F32)),
        in_specs=[spec(VMEM)] * 3,
        out_specs=[spec(VMEM), spec(VMEM)],
        scratch_shapes=[VMEM((2, 2, 4, 8, 8, WIDTH), BF16)] * 4
        + [
            VMEM((2, 4, 16, 8, WIDTH), BF16),
            VMEM((2, 4, 16, 8, WIDTH), BF16),
            VMEM((2, 16, 8, WIDTH), F32),
            VMEM((16, 8, 128), F32),
            DMA((1,)), DMA((41,)), DMA((41,)), DMA((16,)), DMA((16,)),
        ],
        compiler_params=pltpu.CompilerParams(
            collective_id=1, has_side_effects=True, vmem_limit_bytes=20 * 2**20
        ),
    )(sums.reshape(4, 4, 2, 2, 8, 8, WIDTH), own, totals)
    row = lax.dynamic_index_in_dim(class_tot, lax.axis_index("cls") // 8, 0, keepdims=False)
    class_weights = lax.dynamic_slice_in_dim(row, place, 16)
    log_norm = lse[0].reshape(count, CANDS)[:, 0]
    return (class_sums.reshape(groups, 16, WIDTH), class_weights, log_norm)


def solution(mesh):
    in_specs = (
        P(("cls", "prt"), None, None),
        P("cls", None, None),
        P(("cls", "prt"), None),
        P(("cls", "prt"), None, None),
    )
    out_specs = (P("cls", "prt", None), P("cls"), P(("cls", "prt")))
    return jax.shard_map(
        per_device, mesh=mesh, in_specs=in_specs, out_specs=out_specs, check_vma=False
    )
```

```python
import functools
import math

import jax
import jax.numpy as jnp
import numpy as np
from jax import lax
from jax.experimental import pallas as pl
from jax.experimental.pallas import tpu as pltpu
from jax.sharding import PartitionSpec as P

CYCLES = 128
HARM = 256
WIDTH = 2 * HARM
ROTS = 36
OWN_TOP = 4
CAND_OWN = 4
CANDS = OWN_TOP * CAND_OWN
GROUP = 4
ANG = 40
EXT = WIDTH + 128
VMEM, SMEM, HBM = pltpu.VMEM, pltpu.SMEM, pltpu.HBM
F32, BF16 = jnp.float32, jnp.bfloat16
DMA = pltpu.SemaphoreType.DMA
SCALE = 2.0 / math.sqrt(CYCLES * WIDTH)


def split3(x):
    high = x.astype(jnp.bfloat16).astype(np.float32)
    mid = (x - high).astype(jnp.bfloat16).astype(np.float32)
    low = (x - high - mid).astype(jnp.bfloat16).astype(np.float32)
    return high, mid, low


def spectral_tables():
    harmonic = np.arange(HARM, dtype=np.float32)
    angles = np.float32(2.0 * math.pi) * np.arange(ROTS, dtype=np.float32) / np.float32(ROTS)
    phase = (harmonic[:, None] * angles[None, :]).astype(np.float64)
    cos, sin = np.cos(phase).astype(np.float32).T, np.sin(phase).astype(np.float32).T
    forward = np.zeros((ANG, EXT), np.float32)
    forward[:ROTS, :HARM], forward[:ROTS, HARM:WIDTH] = cos, sin
    forward[:ROTS, WIDTH:] = -0.5
    backward = np.zeros((ANG, EXT), np.float32)
    backward[:ROTS, :HARM], backward[:ROTS, HARM:WIDTH] = cos, -sin
    backward[:ROTS, WIDTH:] = 1.0
    f_high, f_mid, f_low = split3(forward)
    b_high, b_mid, b_low = split3(backward)
    fwd = np.concatenate([f_high, f_mid, f_low, np.zeros((8, EXT), np.float32)], 0)
    bwd = np.concatenate([b_high, b_high, b_high, b_mid, b_mid, b_low], 0)
    return jnp.asarray(fwd, BF16), jnp.asarray(bwd, BF16)


def parts3(x):
    high = x.astype(BF16)
    rest = x - high.astype(F32)
    mid = rest.astype(BF16)
    low = (rest - mid.astype(F32)).astype(BF16)
    return high, mid, low


def row_sums(vs):
    row = lax.broadcasted_iota(jnp.int32, vs[0].shape, 0)
    for step in (1, 2, 4):
        keep = (row % (2 * step)) < step
        vs = [
            jnp.where(keep, a, b) + pltpu.roll(jnp.where(keep, b, a), 8 - step, 0)
            for a, b in zip(vs[0::2], vs[1::2])
        ]
    return vs[0]


def group_all(x, op):
    lane = lax.broadcasted_iota(jnp.int32, x.shape, 1)
    n = x.shape[1]
    for step in (1, 2, 4, 8):
        other = jnp.where(
            (lane // step) % 2 == 0, pltpu.roll(x, n - step, 1), pltpu.roll(x, step, 1)
        )
        x = op(x, other)
    return x


def where_am_i():
    cls = lax.axis_index("cls")
    return cls // 8, (cls // 2) % 4, cls % 2, lax.axis_index("prt")


def cls_of(x, y, core):
    return (x % 4) * 8 + (y % 4) * 2 + core


def remote(src, dst, send, recv, cls, prt):
    return pltpu.make_async_remote_copy(
        src, dst, send, recv, device_id=(cls, prt), device_id_type=pl.DeviceIdType.MESH
    )


def greet(peers):
    barrier = pltpu.get_barrier_semaphore()
    for cls, prt in peers:
        pl.semaphore_signal(
            barrier, inc=1, device_id=(cls, prt), device_id_type=pl.DeviceIdType.MESH
        )
    pl.semaphore_wait(barrier, len(peers))


def assign_kernel(
    part, refs, cand, fwd_hbm,
    halves, weights, cand_out, lse_out,
    pbuf, rbuf, rcomb, cbuf, csm, cross, normrow, norms, cout, cin, wown, fwd, lsem, ssem, rsem,
):
    x, y, core, z = where_am_i()
    me = cls_of(x, y, core)
    mate = cls_of(x, y, 1 - core)
    greet(
        [(me, (z + d) % 8) for d in range(1, 8)]
        + [(cls_of(x + d, y, core), z) for d in (1, 3)]
        + [(cls_of(x, y + d, core), z) for d in (1, 3)]
        + [(mate, z)]
    )
    around = (1, 7, 2, 6, 3, 5, 4)

    def at(dx, dy, col=None):
        return cls_of(x - dx + 4, y - dy + 4, core if col is None else col)

    def go(dx, dy):
        return cls_of(x + dx + 4, y + dy + 4, core)

    def piece(g, start=0, size=16):
        return rbuf.at[pl.ds(g * 16 + start, size)]

    sent = []

    def send(src, dst, k, cls, prt):
        cp = remote(src, dst, ssem.at[k], rsem.at[k], cls, prt)
        cp.start()
        sent.append(cp)

    def pass_on(ref, k, cls):
        send(ref, ref, k, cls, z)

    def arrive(ref, k):
        remote(ref, ref, ssem.at[k], rsem.at[k], me, z).wait_recv()

    for d in around:
        send(cand, cbuf.at[z], d, me, (z + d) % 8)
    own_refs = refs.at[:, z]
    for k, dx, dy in ((16, 1, 0), (17, -1, 0), (18, 0, 1), (19, 0, -1)):
        send(own_refs, piece(me), k, go(dx, dy), z)
    send(own_refs, piece(me), 64, mate, z)
    for h in range(2):
        for d in around:
            rows = pl.ds(8 * h, 8)
            send(part.at[rows, (z + d) % 8], pbuf.at[z, rows], 80 + 32 * h + d, me, (z + d) % 8)
    own = [
        pltpu.make_async_copy(cand, cbuf.at[z], lsem.at[0]),
        pltpu.make_async_copy(own_refs, piece(me), lsem.at[1]),
        pltpu.make_async_copy(part.at[:, z], pbuf.at[z], lsem.at[2]),
    ]
    fwd_cp = pltpu.make_async_copy(fwd_hbm, fwd, lsem.at[4])
    for cp in own + [fwd_cp]:
        cp.start()

    def to_mate(dx, dy):
        pass_on(piece(at(dx, dy)), 64 + 4 * dx + dy, mate)

    for k, (dx, dy) in ((16, (1, 0)), (18, (0, 1)), (17, (3, 0)), (19, (0, 3))):
        g = at(dx, dy)
        arrive(piece(g), k)
        if dy == 0:
            pass_on(piece(g, 0 if dx == 1 else 8, 8), 20 + (dx == 3), go(2 - dx, 0))
            pass_on(piece(g, 0, 8), 24 + 2 * (dx - 1), go(0, 1))
            pass_on(piece(g, 0, 8), 25 + 2 * (dx - 1), go(0, -1))
        else:
            pass_on(piece(g, 0 if dy == 1 else 8, 8), 22 + (dy == 3), go(0, 2 - dy))
            pass_on(piece(g, 8, 8), 30 + 2 * (dy - 1), go(1, 0))
            pass_on(piece(g, 8, 8), 31 + 2 * (dy - 1), go(-1, 0))
        to_mate(dx, dy)
    g = at(2, 0)
    arrive(piece(g, 0, 8), 20)
    pass_on(piece(g, 0, 8), 26, go(0, 1))
    pass_on(piece(g, 0, 8), 27, go(0, -1))
    g = at(0, 2)
    arrive(piece(g, 8, 8), 23)
    pass_on(piece(g, 8, 8), 32, go(1, 0))
    pass_on(piece(g, 8, 8), 33, go(-1, 0))
    for m in (1, 3, 2):
        for side in range(2):
            dy = 1 + 2 * side
            g = at(m, dy)
            arrive(piece(g, 0, 8), 24 + 2 * (m - 1) + side)
            pass_on(piece(g, 4 * side, 4), 36 + 2 * (m - 1) + side, go(0, 1 - 2 * side))
            g = at(dy, m)
            arrive(piece(g, 8, 8), 30 + 2 * (m - 1) + side)
            pass_on(piece(g, 8 + 4 * side, 4), 42 + 2 * (m - 1) + side, go(1 - 2 * side, 0))
    arrive(piece(at(2, 0), 8, 8), 21)
    to_mate(2, 0)
    arrive(piece(at(0, 2), 0, 8), 22)
    to_mate(0, 2)
    for dx in (1, 3):
        for dy in (1, 3):
            to_mate(dx, dy)
    for m in (1, 3, 2):
        for side in range(2):
            arrive(piece(at(m, 2), 4 * side, 4), 36 + 2 * (m - 1) + side)
            arrive(piece(at(2, m), 8 + 4 * side, 4), 42 + 2 * (m - 1) + side)
        to_mate(m, 2)
        if m != 2:
            to_mate(2, m)
    for cp in own:
        cp.wait()
    for d in around:
        arrive(cbuf.at[(z - d + 8) % 8], d)
    scp = pltpu.make_async_copy(cbuf, csm, lsem.at[3])
    scp.start()
    c_back = pltpu.make_async_copy(cbuf, cand_out.at[core], lsem.at[0])
    c_back.start()
    send(cbuf, cand_out.at[core], 12, mate, z)

    def norms_of(g):
        @pl.loop(0, 2)
        def _(b):
            vs = []
            for i in range(8):
                k = g * 16 + b * 8 + i
                r = rbuf[k].astype(F32)
                re, im = r[:, :, :HARM], r[:, :, HARM:]
                rcomb[k, 0] = re
                rcomb[k, 1] = re + im
                rcomb[k, 2] = im - re
                s = jnp.sum(re * re + im * im, axis=0)
                vs.append(s[:, :128] + s[:, 128:])
            norms[pl.ds(pl.multiple_of(g * 16 + b * 8, 8), 8), :] = row_sums(vs)

    slices = [(0, 0), (1, 0), (0, 1), (3, 0), (0, 3), (2, 0), (0, 2), (1, 1), (1, 3), (3, 1), (3, 3)]
    slices += [(1, 2), (2, 1), (3, 2), (2, 3), (2, 2)]

    @pl.loop(0, 16)
    def _(k):
        norms_of(2 * k + core)

    for dx, dy in slices:
        arrive(piece(at(dx, dy, 1 - core)), 64 + 4 * dx + dy)

    @pl.loop(0, 16)
    def _(k):
        norms_of(2 * k + 1 - core)

    scp.wait()
    fwd_cp.wait()

    angle = lax.broadcasted_iota(jnp.int32, (ANG, 128), 0)
    used = pl.ds(0, ROTS)

    def score(h, first, last):
        @pl.loop(first, last)
        def _(t):
            d = (t % 2) * ((t + 1) // 2) + (1 - t % 2) * ((8 - t // 2) % 8)
            src = (z - d + 8) % 8

            @pl.when(t > 0)
            def _():
                arrive(pbuf.at[src, pl.ds(8 * h, 8)], 80 + 32 * h + d)

            @pl.loop(0, 8)
            def _(lo):
                p = pbuf[src, h * 8 + lo].astype(F32)
                p_re, p_im = p[:, :, :HARM], p[:, :, HARM:]
                p_sum = p_re + p_im
                for j0 in (0, 8):
                    re, im = [], []
                    row = pl.multiple_of(lo * CANDS + j0, 8)
                    for j in range(8):
                        c = csm[src, h, lo * CANDS + (j0 + j)]
                        k1 = jnp.sum(p_sum * rcomb[c, 0], axis=0)
                        k2 = jnp.sum(p_re * rcomb[c, 1], axis=0)
                        k3 = jnp.sum(p_im * rcomb[c, 2], axis=0)
                        re.append(k1 + k3)
                        im.append(k1 - k2)
                        normrow[pl.ds(lo * CANDS + j0 + j, 1), :] = norms[pl.ds(c, 1), :]
                    cross[pl.ds(row, 8), :HARM] = row_sums(re)
                    cross[pl.ds(row, 8), HARM:WIDTH] = row_sums(im)

            cross[:, WIDTH:] = normrow[...]
            total = jnp.zeros((ANG, 128), F32)
            for part3 in parts3(cross[...]):
                out = lax.dot_general(
                    fwd[...], part3, (((1,), (1,)), ((), ())), preferred_element_type=F32
                )
                total = total + (out[:ANG] + (out[ANG : 2 * ANG] + out[2 * ANG : 3 * ANG]))
            cout[h, d] = total

            @pl.when(t > 0)
            def _():
                k = 88 + 32 * h + d
                remote(cout.at[h, d, used], cin.at[h, d, used], ssem.at[k], rsem.at[k], me, src).start()

    def weigh(h):
        corr = cout[h, 0]
        for d in range(1, 8):
            arrive(cin.at[h, d, used], 88 + 32 * h + d)
            corr = corr + cin[h, d]
        score_h = jnp.where(angle < ROTS, corr * SCALE, -1e30)
        top = group_all(jnp.broadcast_to(jnp.max(score_h, axis=0, keepdims=True), (8, 128)), jnp.maximum)
        expo = jnp.where(angle < ROTS, jnp.exp(score_h - top[:1]), 0.0)
        den = group_all(jnp.broadcast_to(jnp.sum(expo, axis=0, keepdims=True), (8, 128)), jnp.add)
        lse = top + jnp.log(den)
        lse_out[:, 128 * h : 128 * h + 128] = lse
        wown[h] = jnp.where(angle < ROTS, jnp.exp(score_h - lse[:1]), 0.0)
        for d in around:
            send(wown.at[h, used], weights.at[core, z, h, used], 96 + 32 * h + d, me, (z + d) % 8)
        send(wown.at[h, used], weights.at[core, z, h, used], 104 + 32 * h, mate, z)

    score(0, 0, 8)
    score(1, 0, 8)
    weigh(0)
    halves_cp = pltpu.make_async_copy(pbuf.at[:, :, core], halves.at[core], lsem.at[2])
    halves_cp.start()
    send(pbuf.at[:, :, 1 - core], halves.at[core], 13, mate, z)
    weigh(1)
    w_own = pltpu.make_async_copy(wown, weights.at[core, z], lsem.at[1])
    w_own.start()
    for h in range(2):
        for d in around:
            land = weights.at[core, (z - d + 8) % 8, h, used]
            arrive(land, 96 + 32 * h + d)
            pass_on(land, 104 + 32 * h + d, mate)

    for h in range(2):
        for d in range(8):
            arrive(weights.at[1 - core, (z - d + 8) % 8, h, used], 104 + 32 * h + d)
    arrive(cand_out.at[1 - core], 12)
    arrive(halves.at[1 - core], 13)
    for cp in (w_own, c_back, halves_cp):
        cp.wait()
    for cp in sent:
        cp.wait_send()
    for h in range(2):
        for d in range(1, 8):
            k = 88 + 32 * h + d
            remote(cout.at[h, d, used], cin.at[h, d, used], ssem.at[k], rsem.at[k], me, z).wait_send()


def sums_kernel(
    cand_in, halves, w_ref, bwd_hbm,
    out_ref, acc, tot_ref,
    cand, bwd, mixed, tots, accw, lsem,
):
    loads = [
        pltpu.make_async_copy(bwd_hbm, bwd, lsem.at[0]),
        pltpu.make_async_copy(cand_in, cand, lsem.at[1]),
    ]
    for cp in loads:
        cp.start()

    @pl.loop(0, acc.shape[0] // 8)
    def _(c):
        acc[pl.ds(c * 8, 8)] = jnp.zeros((8, 8, WIDTH), F32)

    accw[...] = jnp.zeros_like(accw)
    for cp in loads:
        cp.wait()

    @pl.loop(0, 8)
    def _(pair):
        for b in (2 * pair, 2 * pair + 1):
            w = jnp.concatenate([w_ref[b // 8, b % 8, 0], w_ref[b // 8, b % 8, 1]], 1)
            w = jnp.where(lax.broadcasted_iota(jnp.int32, w.shape, 0) < ROTS, w, 0.0)
            high, mid, low = [v.astype(F32) for v in parts3(w)]
            lhs = jnp.concatenate([high, mid, low, high, mid, high], 0).astype(BF16)
            y = lax.dot_general(
                lhs, bwd[...], (((0,), (0,)), ((), ())), preferred_element_type=F32
            )
            block = pl.ds(b * 16, 16)
            mixed[block] = y[:, :WIDTH].astype(BF16).astype(F32).reshape(16, CANDS, WIDTH)
            tots[block] = y[:, WIDTH:].reshape(16, CANDS, 128)

    @pl.loop(0, 32)
    def _(b):
        @pl.loop(0, 8)
        def _(lo):
            p = halves[b * 8 + lo].astype(F32)
            p_re, p_im = p[:, :HARM], p[:, HARM:]

            def load(j0):
                got = []
                for j in range(j0, j0 + GROUP):
                    c = cand[b, lo * CANDS + j]
                    got.append((c, acc[c, :, :HARM], acc[c, :, HARM:], accw[pl.ds(c, 1), :]))
                return got

            held = load(0)
            for j0 in range(0, CANDS, GROUP):
                new = []
                for j, (c, a_re, a_im, a_tot) in enumerate(held):
                    row = mixed[b * 8 + lo, pl.ds(j0 + j, 1), :]
                    y_re, y_im = row[:, :HARM], row[:, HARM:]
                    new.append(
                        (
                            c,
                            a_re + (p_re * y_re - p_im * y_im),
                            a_im + (p_re * y_im + p_im * y_re),
                            a_tot + tots[b * 8 + lo, pl.ds(j0 + j, 1), :],
                        )
                    )
                if j0 + GROUP < CANDS:
                    held = load(j0 + GROUP)
                for c, re, im, tot in new:
                    acc[c, :, :HARM] = re
                    acc[c, :, HARM:] = im
                    accw[pl.ds(c, 1), :] = tot

    @pl.loop(0, 64)
    def _(c):
        out_ref[pl.ds(c * 8, 8)] = acc[pl.ds(c * 8, 8)].astype(BF16)

    diag = lax.broadcasted_iota(jnp.int32, (128, 128), 0) == lax.broadcasted_iota(
        jnp.int32, (128, 128), 1
    )
    rows = [
        jnp.sum(jnp.where(diag, accw[128 * b : 128 * b + 128, :], 0.0), axis=0, keepdims=True)
        for b in range(4)
    ]
    tot_ref[...] = jnp.concatenate(rows + [jnp.zeros((4, 128), F32)], 0)


def scatter_kernel(
    part, own, tot,
    out_ref, tot_out,
    relay, direct, joined, send3, s2, r2, fin, totin,
    lsem, ssem, rsem, tsend, trecv,
):
    x, y, core, z = where_am_i()
    me = cls_of(x, y, core)
    mate = cls_of(x, y, 1 - core)
    offsets = [(dx, dy) for dx in range(4) for dy in range(4) if dx or dy]
    greet([(cls_of(x + dx, y + dy, core), z) for dx, dy in offsets] + [(mate, z)])
    sent = []

    def send(src, dst, k, cls):
        cp = remote(src, dst, ssem.at[k], rsem.at[k], cls, z)
        cp.start()
        sent.append(cp)

    def arrive(ref, k):
        remote(ref, ref, ssem.at[k], rsem.at[k], me, z).wait_recv()

    def sel(k, to, h):
        to = (to + 8) % 4
        return part.at[to, :, 0, h] if k == 0 else part.at[:, to, 1, h]

    def step(k, d, first):
        along_x = (k == 0) == first
        return cls_of(x + d + 4, y, core) if along_x else cls_of(x, y + d + 4, core)

    for dx, dy in offsets:
        k = 4 * dx + dy
        cp = remote(tot, totin.at[k], tsend.at[k], trecv.at[k], cls_of(x + dx, y + dy, core), z)
        cp.start()
        sent.append(cp)
    for k in range(2):
        u = (x, y)[k]
        send(sel(k, u + 2, 0), relay.at[k, 0], 8 * k, step(k, 1, True))
        send(sel(k, u + 2, 1), relay.at[k, 1], 8 * k + 1, step(k, -1, True))
    for k in range(2):
        u = (x, y)[k]
        send(sel(k, u + 1, 1), direct.at[k, 0], 8 * k + 2, step(k, 1, True))
        send(sel(k, u - 1, 0), direct.at[k, 1], 8 * k + 3, step(k, -1, True))
    def partial(k, to, w, q):
        g = (to % 4) * 8 + w * 2 if k == 0 else w * 8 + (to % 4) * 2 + 1
        return own[g * 16 + q]

    rounds = (2, 1, 3, 0)
    for k in range(2):
        u, v = (x, y)[k], (y, x)[k]
        for side in range(2):
            arrive(relay.at[k, side], 8 * k + side)
        for e in rounds:
            w = (v + e) % 4
            for side in range(2):
                to = u + 1 + 2 * side

                @pl.loop(0, 8)
                def _(q, k=k, w=w, side=side, to=to):
                    send3[k, side, w, q] = (
                        relay[k, side, w, q].astype(F32) + partial(k, to, w, side * 8 + q)
                    ).astype(BF16)

                n = 16 + 8 * k + 2 * e + side
                send(send3.at[k, side, w], joined.at[k, side, w], n, step(k, 1 - 2 * side, True))
    for k in range(2):
        for side in range(2):
            arrive(direct.at[k, side], 8 * k + 2 + side)
    for e in rounds:
        for k in range(2):
            u, v = (x, y)[k], (y, x)[k]
            w = (v + e) % 4
            for side in range(2):
                arrive(joined.at[k, side, w], 16 + 8 * k + 2 * e + side)

            @pl.loop(0, 8)
            def _(q, k=k, u=u, w=w, e=e):
                for side in range(2):
                    total = partial(k, u, w, side * 8 + q) + (
                        joined[k, side, w, q].astype(F32) + direct[k, 1 - side, w, q].astype(F32)
                    )
                    if e:
                        s2[k, e, side * 8 + q] = total.astype(BF16)
                    else:
                        fin[k, side * 8 + q] = total

            if e:
                send(s2.at[k, e], r2.at[k, e], 32 + 4 * k + e, step(k, e, False))
    for k in range(2):
        for e in (1, 2, 3):
            arrive(r2.at[k, e], 32 + 4 * k + e)

        @pl.loop(0, 16)
        def _(q, k=k):
            fin[k, q] = fin[k, q] + (
                (r2[k, 1, q].astype(F32) + r2[k, 2, q].astype(F32)) + r2[k, 3, q].astype(F32)
            )

    send(fin.at[1 - core], out_ref.at[:, core], 40, mate)
    keep = pltpu.make_async_copy(fin.at[core], out_ref.at[:, core], lsem.at[0])
    keep.start()
    total = tot[...]
    for dx, dy in offsets:
        k = 4 * dx + dy
        remote(totin.at[k], totin.at[k], tsend.at[k], trecv.at[k], me, z).wait_recv()
        total = total + totin[k]
    tot_out[...] = total
    arrive(out_ref.at[:, 1 - core], 40)
    keep.wait()
    for cp in sent:
        cp.wait_send()


def spec(space):
    return pl.BlockSpec(memory_space=space)


def sds(shape, dtype):
    return jax.ShapeDtypeStruct(shape, dtype)


def per_device(particles, references, owner_groups, class_order):
    count = particles.shape[0]
    groups = references.shape[0]
    core = lax.axis_index("cls") % 2
    place = lax.axis_index("cls") % 8 // 2 * 32 + core * 16
    fwd, bwd = spectral_tables()
    own_cand = (owner_groups[:, :, None] * groups + class_order[:, :, :CAND_OWN]).reshape(2, 128)

    halves, weights, cand, lse = pl.pallas_call(
        assign_kernel,
        out_shape=(
            sds((2, 8, 16, 8, WIDTH), BF16),
            sds((2, 8, 2, ANG, 128), F32),
            sds((2, 8, 2, 128), jnp.int32),
            sds((8, 256), F32),
        ),
        in_specs=[spec(HBM), spec(HBM), spec(VMEM), spec(HBM)],
        out_specs=[spec(VMEM)] * 4,
        scratch_shapes=[
            VMEM((8, 16, 2, 8, WIDTH), BF16),
            VMEM((512, 2, 8, WIDTH), BF16),
            VMEM((512, 3, 2, 8, HARM), F32),
            VMEM((8, 2, 128), jnp.int32),
            SMEM((8, 2, 128), jnp.int32),
            VMEM((128, EXT), F32),
            VMEM((128, 128), F32),
            VMEM((512, 128), F32),
            VMEM((2, 8, ANG, 128), F32),
            VMEM((2, 8, ANG, 128), F32),
            VMEM((2, ANG, 128), F32),
            VMEM((128, EXT), BF16),
            DMA((5,)), DMA((144,)), DMA((144,)),
        ],
        compiler_params=pltpu.CompilerParams(
            collective_id=0, has_side_effects=True, vmem_limit_bytes=50 * 2**20
        ),
    )(
        particles.reshape(count, 8, 2, 8, WIDTH),
        references.reshape(groups, 8, 2, 8, WIDTH),
        own_cand,
        pltpu.with_memory_space_constraint(fwd, HBM),
    )
    sums, own, totals = pl.pallas_call(
        sums_kernel,
        out_shape=(
            sds((512, 8, WIDTH), BF16),
            sds((512, 8, WIDTH), F32),
            sds((8, 128), F32),
        ),
        in_specs=[spec(VMEM), spec(VMEM), spec(VMEM), spec(HBM)],
        out_specs=[spec(VMEM)] * 3,
        scratch_shapes=[
            SMEM((32, 128), jnp.int32),
            VMEM((6 * ANG, EXT), BF16),
            VMEM((256, CANDS, WIDTH), F32),
            VMEM((256, CANDS, 128), F32),
            VMEM((512, 128), F32),
            DMA((2,)),
        ],
        compiler_params=pltpu.CompilerParams(vmem_limit_bytes=20 * 2**20),
    )(cand.reshape(32, 128), halves.reshape(256, 8, WIDTH), weights, bwd)
    class_sums, class_tot = pl.pallas_call(
        scatter_kernel,
        out_shape=(sds((16, 2, 8, WIDTH), F32), sds((8, 128), F32)),
        in_specs=[spec(VMEM)] * 3,
        out_specs=[spec(VMEM), spec(VMEM)],
        scratch_shapes=[VMEM((2, 2, 4, 8, 8, WIDTH), BF16)] * 4
        + [
            VMEM((2, 4, 16, 8, WIDTH), BF16),
            VMEM((2, 4, 16, 8, WIDTH), BF16),
            VMEM((2, 16, 8, WIDTH), F32),
            VMEM((16, 8, 128), F32),
            DMA((1,)), DMA((41,)), DMA((41,)), DMA((16,)), DMA((16,)),
        ],
        compiler_params=pltpu.CompilerParams(
            collective_id=1, has_side_effects=True, vmem_limit_bytes=20 * 2**20
        ),
    )(sums.reshape(4, 4, 2, 2, 8, 8, WIDTH), own, totals)
    row = lax.dynamic_index_in_dim(class_tot, lax.axis_index("cls") // 8, 0, keepdims=False)
    class_weights = lax.dynamic_slice_in_dim(row, place, 16)
    log_norm = lse[0].reshape(count, CANDS)[:, 0]
    return (class_sums.reshape(groups, 16, WIDTH), class_weights, log_norm)


def solution(mesh):
    in_specs = (
        P(("cls", "prt"), None, None),
        P("cls", None, None),
        P(("cls", "prt"), None),
        P(("cls", "prt"), None, None),
    )
    out_specs = (P("cls", "prt", None), P("cls"), P(("cls", "prt")))
    return jax.shard_map(
        per_device, mesh=mesh, in_specs=in_specs, out_specs=out_specs, check_vma=False
    )
```
